256 devices in a mesh: dp: 32 (over x, z_lo, core), cls: 8 (over y, z_hi).
Axes of the slice: x: 4, y: 4, z: 8 (z_hi: 2, z_lo: 4; z = z_hi * 4 + z_lo), core: 2. Of those that a mesh axis runs over, the one named last changes fastest.
Arguments:
- particles: float32 [2048, 2048], P('dp'), may hold values from -500 to 500
- ctf: float32 [2048, 1024], P('dp'), may hold values from -1 to 1
- references: bfloat16 [32, 2048], P('cls'), may hold values from -0.29882812 to 0.29882812
- noise: float32 [1024], replicated, may hold values from 0.5 to 2
- rotations: int32 [18, 1024], replicated, may hold values from 0 to 1023, each once within a row
- counts: int32 [64], P('dp'), may hold values from 1 to 32, 640 in all
Outputs:
- class_data: float32 [32, 2048], P('cls', 'dp')
- class_weight: float32 [32, 1024], P('cls', 'dp')
- log_evidence: float32 [2048], P('dp')
The draws below stay inside these ranges and needn't reach their ends.
Inputs may be any that keep to these rules, and one draw needn't show every extreme that they name: `rotations`: each row is a permutation of 0 to 1023. The counts sum to 640; some micrograph has exactly 32 particles.
All inputs are finite; a program needn't handle non-finite values. No bound on the sum of `counts` on one device may be relied on, other than what follows from the above.
Results may differ from the reference program's by a relative error of at most 0.0009.
The reference program's roundings to bfloat16 on the way (of `shifted`, `rotated`, `power`, `ctf_square`, `posterior` and `occupancy`) count: a program that leaves them out, or rounds other values in their place, can miss the bound.
Values sent between devices are 32-bit elements; how exact they have to be, the bound alone decides.
A program may use at most 128 MiB of HBM per device.

```python
import math
import jax
import jax.numpy as jnp
import numpy as np
from jax import lax

COEFS = 1024
CLASSES = 32
ROTATIONS = 18
SIDE = 5
SHIFTS = 25
BLOCK = 32
MICS_DEV = 2
MOST = 32
SLOTS = 64
PARTICLE_SLOTS = 2048
MICROGRAPHS = 64
TOTAL = 640
N_DP = 32


def draw_particles(key, part):
    extent = (PARTICLE_SLOTS, 2 * COEFS)
    row_key, entry_key = jax.random.split(jax.random.fold_in(key, 7))
    top_scale = 1000.0 / math.sqrt(COEFS)
    row_scales = jnp.exp(jax.random.uniform(row_key, (PARTICLE_SLOTS, 1), jnp.float32, 0.0, math.log(top_scale)))
    values = jnp.clip(jax.random.normal(entry_key, extent, jnp.float32), -4.0, 4.0) * row_scales
    return values.astype(jnp.float32)


def levels(stream_key, shape, cuts, least, top_value):
    loudness = 1.0
    for axis_at, shards_of in cuts:
        steps = jax.random.uniform(jax.random.fold_in(jax.random.fold_in(stream_key, 6), axis_at), (shards_of,), jnp.float32, least / len(cuts), top_value / len(cuts))
        loudness = loudness * jnp.repeat(jnp.exp(steps), shape[axis_at] // shards_of).reshape((-1,) + (1,) * (len(shape) - 1 - axis_at))
    return loudness


def profile(count, total, bound, slope):
    weights = [(1 << 20) // math.isqrt(rank ** slope) + 1 for rank in range(2, count + 1)]
    spare, given = total - bound - (count - 1), [1] * (count - 1)
    while spare > 0:
        movable = [i for i in range(count - 1) if given[i] < bound]
        whole, budget = sum([weights[i] for i in movable]), spare
        for i in movable:
            more = min(bound - given[i], max(1, budget * weights[i] // whole), spare)
            given[i] = given[i] + more
            spare = spare - more
    return np.array([bound] + given)


def ragged(rng, number_of, total, most, slope):
    if number_of == 2:
        one = jax.random.randint(rng, (), max(1, total - most), min(most, total - 1) + 1)
        return jnp.stack([one, total - one])
    lengths = jnp.asarray(profile(number_of, total, most, slope), jnp.int32)
    couples = (number_of - 1) // 2
    donor, sink = lengths[1:1 + 2 * couples:2], lengths[2:2 + 2 * couples:2]
    room = jnp.minimum(donor - 1, most - sink)
    passed = jax.random.randint(jax.random.fold_in(rng, 1), (couples,), 0, 1 << 20) % (room + 1)
    lengths = lengths.at[1:1 + 2 * couples:2].set(donor - passed).at[2:2 + 2 * couples:2].set(sink + passed)
    return lengths[jax.random.permutation(jax.random.fold_in(rng, 2), number_of)]


def scatter_about(own_key, dims, spread, reach, cuts=(), held_as=jnp.bfloat16):
    loudness = levels(own_key, dims, cuts, -0.22, 0.18) if cuts else 1.0
    result = jax.random.normal(own_key, dims, jnp.float32) * spread * loudness
    return jnp.minimum(jnp.maximum(result, -reach), reach).astype(held_as)


def setup_inputs(seed: int = 0) -> dict:
    key_list = jax.random.split(jax.random.key(seed), 7)
    return {
        "particles": draw_particles(jax.random.fold_in(key_list[6], 71), 0),
        "ctf": jnp.clip(jax.random.uniform(key_list[1], (PARTICLE_SLOTS, COEFS), jnp.float32, -1.0, 1.0) * levels(key_list[1], (PARTICLE_SLOTS, COEFS), ((0, 32),), -0.4, 0.0), -1.0, 1.0),
        "references": scatter_about(key_list[2], (CLASSES, 2 * COEFS), 0.05, 0.29882812, ((0, 8),)),
        "noise": jnp.clip(jnp.exp(jax.random.uniform(key_list[3], (COEFS,), jnp.float32, math.log(0.5), math.log(2.0))), 0.5, 2.0),
        "rotations": jax.vmap(lambda own: jax.random.permutation(own, COEFS))(jax.random.split(key_list[4], ROTATIONS)).reshape((ROTATIONS, COEFS)).astype(jnp.int32),
        "counts": ragged(key_list[5], MICROGRAPHS, TOTAL, MOST, 2).astype(jnp.int32),
    }


def phase_tables(coef_count):
    coefs = jnp.arange(coef_count)
    freq_x = (coefs % 32).astype(jnp.float32)
    freq_y = (coefs // 32 - coef_count // 64).astype(jnp.float32)
    offsets = jnp.arange(SHIFTS)
    step_x = (offsets // SIDE - SIDE // 2).astype(jnp.float32)
    step_y = (offsets % SIDE - SIDE // 2).astype(jnp.float32)
    angles = (2.0 * math.pi / 64.0) * (step_x[:, None] * freq_x[None, :] + step_y[:, None] * freq_y[None, :])
    return jnp.cos(angles), jnp.sin(angles)


def rotate_refs(refs, rotations):
    class_count = refs.shape[0]
    turn_count, coef_count = rotations.shape
    halves = refs.reshape(class_count, 2, coef_count)
    picked = halves[:, :, rotations]
    return jnp.transpose(picked, (0, 2, 1, 3)).reshape(class_count * turn_count, 2 * coef_count)


def inverse_rotations(rotations):
    turn_count, coef_count = rotations.shape
    return jnp.zeros((turn_count, coef_count), jnp.int32).at[jnp.arange(turn_count)[:, None], rotations].set(jnp.arange(coef_count, dtype=jnp.int32)[None, :])


def ref_power(rotated, noise):
    coef_count = noise.shape[0]
    widened = rotated.astype(jnp.float32)
    return ((widened[:, :coef_count] * widened[:, :coef_count] + widened[:, coef_count:] * widened[:, coef_count:]) / noise[None, :]).astype(jnp.bfloat16)


def block_scores(rows_x, rows_c, rotated, power, noise, cosine_table, sine_table):
    coef_count = noise.shape[0]
    row_count = rows_x.shape[0]
    scaled = rows_x * jnp.concatenate([rows_c, rows_c], 1) / jnp.concatenate([noise, noise])[None, :]
    real_part = scaled[:, None, :coef_count]
    imag_part = scaled[:, None, coef_count:]
    shifted = jnp.concatenate([real_part * cosine_table[None] + imag_part * sine_table[None], imag_part * cosine_table[None] - real_part * sine_table[None]], 2)
    shifted = shifted.astype(jnp.bfloat16).reshape(row_count * SHIFTS, 2 * coef_count)
    ctf_square = (rows_c * rows_c).astype(jnp.bfloat16)
    cross = jnp.dot(shifted, rotated.T, preferred_element_type=jnp.float32).reshape(row_count, SHIFTS, -1)
    penalty = jnp.dot(ctf_square, power.T, preferred_element_type=jnp.float32)
    return cross - 0.5 * penalty[:, None, :], shifted, ctf_square


def accumulate(scores, evidence, shifted, ctf_square, weighted, ctf_weight):
    posterior = jnp.exp(scores - evidence[:, None, None]).astype(jnp.bfloat16)
    flat = posterior.reshape(-1, posterior.shape[2])
    weighted = weighted + jnp.dot(flat.T, shifted, preferred_element_type=jnp.float32)
    occupancy = jnp.sum(posterior.astype(jnp.float32), axis=1).astype(jnp.bfloat16)
    ctf_weight = ctf_weight + jnp.dot(occupancy.T, ctf_square, preferred_element_type=jnp.float32)
    return weighted, ctf_weight


def unrotate(terms, inverse, class_count):
    turn_count, coef_count = inverse.shape
    layered = terms.reshape(class_count, turn_count, -1, coef_count)
    return jnp.sum(jnp.take_along_axis(layered, inverse[None, :, None, :], axis=3), axis=1).reshape(class_count, -1)


def reference(particles, ctf, references, noise, rotations, counts):
    cosine_table, sine_table = phase_tables(COEFS)
    rotated = rotate_refs(references, rotations)
    power = ref_power(rotated, noise)
    loads = jnp.sum(counts.reshape(N_DP, MICS_DEV), axis=1)
    places = jnp.arange(PARTICLE_SLOTS)
    live = (places % SLOTS) < loads[places // SLOTS]
    order = jnp.argsort(jnp.where(live, 0, 1).astype(jnp.int32), stable=True)[:TOTAL].astype(jnp.int32)
    rows_x = particles[order].reshape(TOTAL // BLOCK, BLOCK, 2 * COEFS)
    rows_c = ctf[order].reshape(TOTAL // BLOCK, BLOCK, COEFS)
    pair_count = rotated.shape[0]

    def one_block(carry, pieces):
        weighted, ctf_weight = carry
        scores, shifted, ctf_square = block_scores(pieces[0], pieces[1], rotated, power, noise, cosine_table, sine_table)
        peak_score = jnp.max(scores, axis=(1, 2))
        evidence = peak_score + jnp.log(jnp.sum(jnp.exp(scores - peak_score[:, None, None]), axis=(1, 2)))
        weighted, ctf_weight = accumulate(scores, evidence, shifted, ctf_square, weighted, ctf_weight)
        return (weighted, ctf_weight), evidence

    start_sums = (jnp.zeros((pair_count, 2 * COEFS), jnp.float32), jnp.zeros((pair_count, COEFS), jnp.float32))
    (weighted, ctf_weight), evidence = lax.scan(one_block, start_sums, (rows_x, rows_c))
    log_evidence = jnp.zeros((PARTICLE_SLOTS,), jnp.float32).at[order].set(evidence.reshape(-1))
    inverse = inverse_rotations(rotations)
    class_data = unrotate(weighted, inverse, CLASSES)
    class_weight = unrotate(ctf_weight / noise[None, :], inverse, CLASSES)
    return class_data, class_weight, log_evidence
```

```python
import functools
import math

import jax
import jax.numpy as jnp
import numpy as np
from jax import lax
from jax.experimental import pallas as pl
from jax.experimental.pallas import tpu as pltpu
from jax.sharding import PartitionSpec as P

SIDE = 5
SHIFTS = 25
LANES = 128
TURNS = 18
QPAD = 80
MESH = pl.DeviceIdType.MESH


def phase_tables(coef_count, rows):
    coefs = np.arange(coef_count)
    freq_x = (coefs % 32).astype(np.float32)
    freq_y = (coefs // 32 - coef_count // 64).astype(np.float32)
    offsets = np.arange(SHIFTS)
    step_x = (offsets // SIDE - SIDE // 2).astype(np.float32)
    step_y = (offsets % SIDE - SIDE // 2).astype(np.float32)
    angles = np.float32(2.0 * math.pi / 64.0) * (
        step_x[:, None] * freq_x[None, :] + step_y[:, None] * freq_y[None, :]
    )
    wide = angles.astype(np.float32).astype(np.float64)
    pad = ((0, rows - SHIFTS), (0, 0))
    return (
        np.pad(np.cos(wide).astype(np.float32), pad),
        np.pad(np.sin(wide).astype(np.float32), pad),
    )


def iota(shape, axis):
    return lax.broadcasted_iota(jnp.int32, shape, axis)


def lane_take(values, index):
    return jnp.take_along_axis(values, index, axis=1, mode="promise_in_bounds")


def kernel(
    dims,
    counts_ref,
    part_ref,
    ctf_ref,
    refs_ref,
    noise_ref,
    rot_ref,
    cos_ref,
    sin_ref,
    data_ref,
    weight_ref,
    evid_ref,
    scaled,
    csq,
    shifted,
    rotated,
    scores,
    weighted,
    inverse,
    turns,
    total,
    stat_send,
    stat_recv,
    piece_send,
    piece_recv,
    stat_sems,
    piece_sems,
):
    n_dp, n_cls, slots, coefs = dims
    tiles = coefs // LANES
    pairs = TURNS // 2
    shift_rows = shifted.shape[0]
    lanes_used = SHIFTS * slots
    me_dp = lax.axis_index("dp")
    me_cls = lax.axis_index("cls")

    barrier = pltpu.get_barrier_semaphore()

    def greet_dp(o, c):
        pl.semaphore_signal(
            barrier, inc=1, device_id=(lax.rem(me_dp + o, n_dp), me_cls), device_id_type=MESH
        )
        return c

    def greet_cls(o, c):
        pl.semaphore_signal(
            barrier, inc=1, device_id=(me_dp, lax.rem(me_cls + o, n_cls)), device_id_type=MESH
        )
        return c

    lax.fori_loop(1, n_dp, greet_dp, 0)
    lax.fori_loop(1, n_cls, greet_cls, 0)

    noise = noise_ref[...]
    transfer = ctf_ref[...]
    scaled[:, :coefs] = part_ref[:, :coefs] * transfer / noise
    scaled[:, coefs:] = part_ref[:, coefs:] * transfer / noise
    csq[...] = (transfer * transfer).astype(jnp.bfloat16)

    def one_shift(s, c):
        cosine = cos_ref[pl.ds(s, 1), :]
        sine = sin_ref[pl.ds(s, 1), :]
        rows = pl.ds(pl.multiple_of(s * slots, slots), slots)
        real = scaled[:, :coefs]
        imag = scaled[:, coefs:]
        shifted[rows, :coefs] = (real * cosine + imag * sine).astype(jnp.bfloat16)
        shifted[rows, coefs:] = (imag * cosine - real * sine).astype(jnp.bfloat16)
        return c

    lax.fori_loop(0, shift_rows // slots, one_shift, 0)

    low_half = iota((8, LANES), 0) < 4
    for r in range(TURNS):
        turns[r] = jnp.broadcast_to(rot_ref[r : r + 1, :], (8, coefs))
    refs4 = refs_ref[...].astype(jnp.float32)
    total[:, : 2 * coefs] = jnp.concatenate([refs4, refs4], axis=0)

    def rotate_pair(p, c):
        rows = pl.ds(pl.multiple_of(p * 8, 8), 8)
        for j in range(tiles):
            cols = slice(j * LANES, (j + 1) * LANES)
            index = jnp.where(low_half, turns[2 * p, :, cols], turns[2 * p + 1, :, cols])
            lane = index & (LANES - 1)
            tile = lax.shift_right_logical(index, 7)
            for part in range(2):
                found = jnp.zeros((8, LANES), jnp.float32)
                for s in range(tiles):
                    base = part * coefs + s * LANES
                    picked = lane_take(total[:, base : base + LANES], lane)
                    found = jnp.where(tile == s, picked, found)
                base = part * coefs + j * LANES
                rotated[rows, base : base + LANES] = found
        return c

    lax.fori_loop(0, pairs, rotate_pair, 0)
    rot_rows = rotated.shape[0]
    turned = rotated[...]
    power = (
        (turned[:, :coefs] * turned[:, :coefs] + turned[:, coefs:] * turned[:, coefs:]) / noise
    ).astype(jnp.bfloat16)
    pad_rows = jnp.zeros((QPAD - rot_rows, 2 * coefs), jnp.float32)
    turned = jnp.concatenate([turned, pad_rows], axis=0).astype(jnp.bfloat16)
    squares = csq[...]
    contract_cols = (((1,), (1,)), ((), ()))
    penalty = lax.dot_general(
        power,
        jnp.concatenate([squares, squares], axis=0),
        contract_cols,
        preferred_element_type=jnp.float32,
    )
    half_penalty = 0.5 * penalty

    lane_row = iota((1, LANES), 1)
    peak = jnp.full((1, LANES), -jnp.inf, jnp.float32)
    chunks = shift_rows // LANES
    for j in range(chunks):
        block = shifted[j * LANES : (j + 1) * LANES, :]
        cross = lax.dot_general(
            turned, block, contract_cols, preferred_element_type=jnp.float32
        )[:rot_rows]
        values = cross - half_penalty
        if (j + 1) * LANES > lanes_used:
            values = jnp.where(j * LANES + lane_row < lanes_used, values, -1e30)
        scores[:, j * LANES : (j + 1) * LANES] = values
        peak = jnp.maximum(peak, jnp.max(values, axis=0, keepdims=True))
    peak = jnp.maximum(peak, pltpu.roll(peak, slots, 1))
    mass = jnp.zeros((1, LANES), jnp.float32)
    for j in range(chunks):
        cols = slice(j * LANES, (j + 1) * LANES)
        values = jnp.exp(scores[:, cols] - peak)
        if (j + 1) * LANES > lanes_used:
            values = jnp.where(j * LANES + lane_row < lanes_used, values, 0.0)
        scores[:, cols] = values
        mass = mass + jnp.sum(values, axis=0, keepdims=True)
    mass = mass + pltpu.roll(mass, slots, 1)
    stat_send[...] = jnp.where(iota((8, LANES), 0) == 0, peak, mass)

    pl.semaphore_wait(barrier, n_dp - 1 + n_cls - 1)

    def stat_copy(o):
        return pltpu.make_async_remote_copy(
            src_ref=stat_send,
            dst_ref=stat_recv.at[o - 1],
            send_sem=stat_sems.at[0],
            recv_sem=stat_sems.at[1],
            device_id=(me_dp, lax.rem(me_cls + o, n_cls)),
            device_id_type=MESH,
        )

    def stat_start(o, c):
        stat_copy(o).start()
        return c

    lax.fori_loop(1, n_cls, stat_start, 0)

    place = iota((1, coefs), 1)
    place_low = (place & (LANES - 1)).astype(jnp.float32)
    place_high = lax.shift_right_logical(place, 7).astype(jnp.float32)

    def invert(r, c):
        row = turns[r, 0:1, :]
        lane = row & (LANES - 1)
        tile = lax.shift_right_logical(row, 7)
        hot = jnp.where(iota((LANES, coefs), 0) == lane, 1.0, 0.0).astype(jnp.bfloat16)
        mine = iota((tiles, coefs), 0) == tile
        source = jnp.concatenate(
            [jnp.where(mine, place_low, 0.0), jnp.where(mine, place_high, 0.0)], axis=0
        ).astype(jnp.bfloat16)
        inverse[r] = lax.dot_general(
            source, hot, contract_cols, preferred_element_type=jnp.float32
        ).astype(jnp.int32)
        return c

    lax.fori_loop(0, TURNS, invert, 0)

    pltpu.make_async_copy(stat_recv, stat_recv, stat_sems.at[1]).wait()
    pltpu.make_async_copy(stat_recv, stat_recv, stat_sems.at[0]).wait()

    top = peak
    for o in range(n_cls - 1):
        top = jnp.maximum(top, stat_recv[o, 0:1, :])
    sums = mass * jnp.exp(peak - top)
    for o in range(n_cls - 1):
        sums = sums + stat_recv[o, 1:2, :] * jnp.exp(stat_recv[o, 0:1, :] - top)
    evidence = top + jnp.log(sums)
    live = (lane_row & (slots - 1)) < counts_ref[0] + counts_ref[1]
    factor = jnp.where(live, jnp.exp(peak - evidence), 0.0)
    evid_ref[...] = jnp.where(live, evidence, 0.0)[:, :slots]

    occupancy = jnp.zeros((rot_rows, LANES), jnp.float32)
    posterior = []
    for j in range(chunks):
        cols = slice(j * LANES, (j + 1) * LANES)
        values = (scores[:, cols] * factor).astype(jnp.bfloat16).astype(jnp.float32)
        occupancy = occupancy + values
        posterior.append(
            jnp.concatenate(
                [values, jnp.zeros((QPAD - rot_rows, LANES), jnp.float32)], axis=0
            ).astype(jnp.bfloat16)
        )
    posterior = jnp.concatenate(posterior, axis=1)
    weighted[:, : 2 * coefs] = lax.dot_general(
        posterior,
        shifted[...],
        (((1,), (0,)), ((), ())),
        preferred_element_type=jnp.float32,
    )[:rot_rows]
    occupancy = occupancy + pltpu.roll(occupancy, slots, 1)
    occupancy = jnp.where(lane_row < slots, occupancy, 0.0)
    occupancy = jnp.concatenate(
        [occupancy, jnp.zeros((QPAD - rot_rows, LANES), jnp.float32)], axis=0
    ).astype(jnp.bfloat16)
    weighted[:, 2 * coefs :] = (
        lax.dot_general(
            occupancy,
            jnp.concatenate([squares, squares], axis=0),
            (((1,), (0,)), ((), ())),
            preferred_element_type=jnp.float32,
        )[:rot_rows]
        / noise
    )

    total[...] = jnp.zeros_like(total)

    def unrotate_pair(p, c):
        rows = pl.ds(pl.multiple_of(p * 8, 8), 8)
        for j in range(tiles):
            lane = jnp.where(
                low_half, inverse[2 * p, j : j + 1, :], inverse[2 * p + 1, j : j + 1, :]
            )
            tile = jnp.where(
                low_half,
                inverse[2 * p, tiles + j : tiles + j + 1, :],
                inverse[2 * p + 1, tiles + j : tiles + j + 1, :],
            )
            for part in range(3):
                found = jnp.zeros((8, LANES), jnp.float32)
                for s in range(tiles):
                    base = part * coefs + s * LANES
                    picked = lane_take(weighted[rows, base : base + LANES], lane)
                    found = jnp.where(tile == s, picked, found)
                base = part * coefs + j * LANES
                total[:, base : base + LANES] += found
        return c

    lax.fori_loop(0, pairs, unrotate_pair, 0)

    n_pieces = n_dp // 2
    for e in range(n_pieces):
        data = total[:, e * LANES : (e + 1) * LANES]
        base = 2 * coefs + (e // 2) * LANES
        mass_tile = total[:, base : base + LANES]
        data = data + pltpu.roll(data, 4, 0)
        mass_tile = mass_tile + pltpu.roll(mass_tile, 4, 0)
        piece_send[e] = jnp.where(low_half, data, mass_tile)

    def piece_start(o, c):
        target = lax.rem(me_dp + o, n_dp)
        pltpu.make_async_remote_copy(
            src_ref=piece_send.at[lax.div(target, 2)],
            dst_ref=piece_recv.at[o - 1],
            send_sem=piece_sems.at[0],
            recv_sem=piece_sems.at[1],
            device_id=(target, me_cls),
            device_id_type=MESH,
        ).start()
        return c

    lax.fori_loop(1, n_dp, piece_start, 0)
    pltpu.make_async_copy(piece_recv, piece_recv, piece_sems.at[1]).wait()
    gathered = piece_send[lax.div(me_dp, 2)]
    for o in range(n_dp - 1):
        gathered = gathered + piece_recv[o]
    data_part = lax.rem(me_dp, 2)
    weight_part = lax.rem(me_dp, 4)
    data_out = jnp.where(data_part == 0, gathered, pltpu.roll(gathered, 64, 1))
    data_ref[...] = data_out[0:4, :64]
    weight_out = gathered
    for w in range(1, 4):
        weight_out = jnp.where(weight_part == w, pltpu.roll(gathered, LANES - 32 * w, 1), weight_out)
    weight_ref[...] = weight_out[4:8, :32]
    pltpu.make_async_copy(piece_recv, piece_recv, piece_sems.at[0]).wait()


def body(particles, ctf, references, noise, rotations, counts):
    slots, coefs = ctf.shape
    classes = references.shape[0]
    n_dp = lax.axis_size("dp")
    n_cls = lax.axis_size("cls")
    padded = SHIFTS + 1
    cosine, sine = phase_tables(coefs, padded)
    rows = padded * slots
    pair_count = classes * TURNS
    vmem = pl.BlockSpec(memory_space=pltpu.VMEM)
    data, weight, evidence = pl.pallas_call(
        functools.partial(kernel, (n_dp, n_cls, slots, coefs)),
        out_shape=(
            jax.ShapeDtypeStruct((classes, 2 * coefs // n_dp), jnp.float32),
            jax.ShapeDtypeStruct((classes, coefs // n_dp), jnp.float32),
            jax.ShapeDtypeStruct((1, slots), jnp.float32),
        ),
        in_specs=[pl.BlockSpec(memory_space=pltpu.SMEM)] + [vmem] * 7,
        out_specs=(vmem, vmem, vmem),
        scratch_shapes=[
            pltpu.VMEM((slots, 2 * coefs), jnp.float32),
            pltpu.VMEM((slots, coefs), jnp.bfloat16),
            pltpu.VMEM((rows, 2 * coefs), jnp.bfloat16),
            pltpu.VMEM((pair_count, 2 * coefs), jnp.float32),
            pltpu.VMEM((pair_count, rows), jnp.float32),
            pltpu.VMEM((pair_count, 3 * coefs), jnp.float32),
            pltpu.VMEM((TURNS, 2 * coefs // LANES, LANES), jnp.int32),
            pltpu.VMEM((TURNS, 8, coefs), jnp.int32),
            pltpu.VMEM((8, 3 * coefs), jnp.float32),
            pltpu.VMEM((8, LANES), jnp.float32),
            pltpu.VMEM((n_cls - 1, 8, LANES), jnp.float32),
            pltpu.VMEM((n_dp // 2, 8, LANES), jnp.float32),
            pltpu.VMEM((n_dp - 1, 8, LANES), jnp.float32),
            pltpu.SemaphoreType.DMA((2,)),
            pltpu.SemaphoreType.DMA((2,)),
        ],
        compiler_params=pltpu.CompilerParams(
            collective_id=0, has_side_effects=True, vmem_limit_bytes=48 << 20
        ),
        name="class_average",
    )(
        counts,
        particles,
        ctf,
        references,
        noise.reshape(1, coefs),
        rotations,
        jnp.asarray(cosine),
        jnp.asarray(sine),
    )
    return data, weight, evidence.reshape(slots)


def solution(mesh):
    placed = (P("dp", None), P("dp", None), P("cls", None), P(), P(), P("dp"))
    return jax.shard_map(
        body,
        mesh=mesh,
        in_specs=placed,
        out_specs=(P("cls", "dp"), P("cls", "dp"), P("dp")),
        check_vma=False,
    )
```

```python
import functools
import math

import jax
import jax.numpy as jnp
import numpy as np
from jax import lax
from jax.experimental import pallas as pl
from jax.experimental.pallas import tpu as pltpu
from jax.sharding import PartitionSpec as P

SIDE = 5
SHIFTS = 25
LANES = 128
TURNS = 18
QPAD = 80
MESH = pl.DeviceIdType.MESH


def phase_tables(coef_count, rows):
    coefs = np.arange(coef_count)
    freq_x = (coefs % 32).astype(np.float32)
    freq_y = (coefs // 32 - coef_count // 64).astype(np.float32)
    offsets = np.arange(SHIFTS)
    step_x = (offsets // SIDE - SIDE // 2).astype(np.float32)
    step_y = (offsets % SIDE - SIDE // 2).astype(np.float32)
    angles = np.float32(2.0 * math.pi / 64.0) * (
        step_x[:, None] * freq_x[None, :] + step_y[:, None] * freq_y[None, :]
    )
    wide = angles.astype(np.float32).astype(np.float64)
    pad = ((0, rows - SHIFTS), (0, 0))
    return (
        np.pad(np.cos(wide).astype(np.float32), pad),
        np.pad(np.sin(wide).astype(np.float32), pad),
    )


def iota(shape, axis):
    return lax.broadcasted_iota(jnp.int32, shape, axis)


def lane_take(values, index):
    return jnp.take_along_axis(values, index, axis=1, mode="promise_in_bounds")


def kernel(
    dims,
    counts_hbm,
    part_hbm,
    ctf_hbm,
    refs_hbm,
    noise_hbm,
    rot_hbm,
    trig_hbm,
    data_ref,
    weight_ref,
    evid_ref,
    counts_ref,
    part_ref,
    ctf_ref,
    refs_ref,
    noise_ref,
    rot_ref,
    trig_ref,
    scaled,
    csq,
    shifted,
    rotated,
    scores,
    weighted,
    inverse,
    turns,
    total,
    stat_send,
    stat_recv,
    piece_weight,
    piece_send,
    piece_recv,
    load_sems,
    stat_sems,
    piece_sems,
):
    n_dp, n_cls, slots, coefs = dims
    tiles = coefs // LANES
    pairs = TURNS // 2
    shift_rows = shifted.shape[0]
    lanes_used = SHIFTS * slots
    me_dp = lax.axis_index("dp")
    me_cls = lax.axis_index("cls")

    loads = [
        pltpu.make_async_copy(source, target, load_sems.at[i])
        for i, (source, target) in enumerate(
            (
                (rot_hbm, rot_ref),
                (refs_hbm, refs_ref),
                (noise_hbm, noise_ref),
                (part_hbm, part_ref),
                (ctf_hbm, ctf_ref),
                (trig_hbm, trig_ref),
                (counts_hbm, counts_ref),
            )
        )
    ]
    for load in loads:
        load.start()

    barrier = pltpu.get_barrier_semaphore()

    def greet_dp(o, c):
        pl.semaphore_signal(
            barrier, inc=1, device_id=(lax.rem(me_dp + o, n_dp), me_cls), device_id_type=MESH
        )
        return c

    def greet_cls(o, c):
        pl.semaphore_signal(
            barrier, inc=1, device_id=(me_dp, lax.rem(me_cls + o, n_cls)), device_id_type=MESH
        )
        return c

    lax.fori_loop(1, n_dp, greet_dp, 0)
    lax.fori_loop(1, n_cls, greet_cls, 0)

    for load in loads:
        load.wait()

    noise = noise_ref[...]
    transfer = ctf_ref[...]
    scaled[:, :coefs] = part_ref[:, :coefs] * transfer / noise
    scaled[:, coefs:] = part_ref[:, coefs:] * transfer / noise
    csq[...] = (transfer * transfer).astype(jnp.bfloat16)

    def one_shift(s, c):
        cosine = trig_ref[s, 0:1, :]
        sine = trig_ref[s, 1:2, :]
        rows = pl.ds(pl.multiple_of(s * slots, slots), slots)
        real = scaled[:, :coefs]
        imag = scaled[:, coefs:]
        shifted[rows, :coefs] = (real * cosine + imag * sine).astype(jnp.bfloat16)
        shifted[rows, coefs:] = (imag * cosine - real * sine).astype(jnp.bfloat16)
        return c

    lax.fori_loop(0, shift_rows // slots, one_shift, 0)

    low_half = iota((8, LANES), 0) < 4
    for r in range(TURNS):
        turns[r] = jnp.broadcast_to(rot_ref[r : r + 1, :], (8, coefs))
    refs4 = refs_ref[...].astype(jnp.float32)
    total[...] = jnp.concatenate([refs4, refs4], axis=0)

    def rotate_pair(p, c):
        rows = pl.ds(pl.multiple_of(p * 8, 8), 8)
        for j in range(tiles):
            cols = slice(j * LANES, (j + 1) * LANES)
            index = jnp.where(low_half, turns[2 * p, :, cols], turns[2 * p + 1, :, cols])
            lane = index & (LANES - 1)
            tile = lax.shift_right_logical(index, 7)
            for part in range(2):
                found = jnp.zeros((8, LANES), jnp.float32)
                for s in range(tiles):
                    base = part * coefs + s * LANES
                    picked = lane_take(total[:, base : base + LANES], lane)
                    found = jnp.where(tile == s, picked, found)
                base = part * coefs + j * LANES
                rotated[rows, base : base + LANES] = found
        return c

    lax.fori_loop(0, pairs, rotate_pair, 0)
    rot_rows = rotated.shape[0]
    turned = rotated[...]
    power = (
        (turned[:, :coefs] * turned[:, :coefs] + turned[:, coefs:] * turned[:, coefs:]) / noise
    ).astype(jnp.bfloat16)
    pad_rows = jnp.zeros((QPAD - rot_rows, 2 * coefs), jnp.float32)
    turned = jnp.concatenate([turned, pad_rows], axis=0).astype(jnp.bfloat16)
    squares = csq[...]
    contract_cols = (((1,), (1,)), ((), ()))
    penalty = lax.dot_general(
        power,
        jnp.concatenate([squares, squares], axis=0),
        contract_cols,
        preferred_element_type=jnp.float32,
    )
    half_penalty = 0.5 * penalty

    lane_row = iota((1, LANES), 1)
    peak = jnp.full((1, LANES), -jnp.inf, jnp.float32)
    chunks = shift_rows // LANES
    for j in range(chunks):
        block = shifted[j * LANES : (j + 1) * LANES, :]
        cross = lax.dot_general(
            turned, block, contract_cols, preferred_element_type=jnp.float32
        )[:rot_rows]
        values = cross - half_penalty
        if (j + 1) * LANES > lanes_used:
            values = jnp.where(j * LANES + lane_row < lanes_used, values, -1e30)
        scores[:, j * LANES : (j + 1) * LANES] = values
        peak = jnp.maximum(peak, jnp.max(values, axis=0, keepdims=True))
    peak = jnp.maximum(peak, pltpu.roll(peak, slots, 1))
    mass = jnp.zeros((1, LANES), jnp.float32)
    for j in range(chunks):
        cols = slice(j * LANES, (j + 1) * LANES)
        values = jnp.exp(scores[:, cols] - peak)
        if (j + 1) * LANES > lanes_used:
            values = jnp.where(j * LANES + lane_row < lanes_used, values, 0.0)
        scores[:, cols] = values
        mass = mass + jnp.sum(values, axis=0, keepdims=True)
    mass = mass + pltpu.roll(mass, slots, 1)
    stat_send[...] = jnp.where(iota((8, LANES), 0) == 0, peak, mass)

    pl.semaphore_wait(barrier, n_dp - 1 + n_cls - 1)

    def stat_copy(o):
        return pltpu.make_async_remote_copy(
            src_ref=stat_send,
            dst_ref=stat_recv.at[o - 1],
            send_sem=stat_sems.at[0],
            recv_sem=stat_sems.at[1],
            device_id=(me_dp, lax.rem(me_cls + o, n_cls)),
            device_id_type=MESH,
        )

    def stat_start(o, c):
        stat_copy(o).start()
        return c

    lax.fori_loop(1, n_cls, stat_start, 0)

    place = iota((1, coefs), 1)
    place_low = (place & (LANES - 1)).astype(jnp.float32)
    place_high = lax.shift_right_logical(place, 7).astype(jnp.float32)

    def invert(r):
        row = turns[r, 0:1, :]
        lane = row & (LANES - 1)
        tile = lax.shift_right_logical(row, 7)
        hot = jnp.where(iota((LANES, coefs), 0) == lane, 1.0, 0.0).astype(jnp.bfloat16)
        mine = iota((tiles, coefs), 0) == tile
        source = jnp.concatenate(
            [jnp.where(mine, place_low, 0.0), jnp.where(mine, place_high, 0.0)], axis=0
        ).astype(jnp.bfloat16)
        return lax.dot_general(
            source, hot, contract_cols, preferred_element_type=jnp.float32
        ).astype(jnp.int32)

    def invert_pair(p, c):
        first = invert(2 * p)
        second = invert(2 * p + 1)
        for j in range(2 * tiles):
            inverse[p, j] = jnp.where(low_half, first[j : j + 1], second[j : j + 1])
        return c

    lax.fori_loop(0, pairs, invert_pair, 0, unroll=3)

    pltpu.make_async_copy(stat_recv, stat_recv, stat_sems.at[1]).wait()
    pltpu.make_async_copy(stat_recv, stat_recv, stat_sems.at[0]).wait()

    top = peak
    for o in range(n_cls - 1):
        top = jnp.maximum(top, stat_recv[o, 0:1, :])
    sums = mass * jnp.exp(peak - top)
    for o in range(n_cls - 1):
        sums = sums + stat_recv[o, 1:2, :] * jnp.exp(stat_recv[o, 0:1, :] - top)
    evidence = top + jnp.log(sums)
    live = (lane_row & (slots - 1)) < counts_ref[0] + counts_ref[1]
    factor = jnp.where(live, jnp.exp(peak - evidence), 0.0)
    evid_ref[...] = jnp.where(live, evidence, 0.0)[:, :slots]

    occupancy = jnp.zeros((rot_rows, LANES), jnp.float32)
    posterior = []
    for j in range(chunks):
        cols = slice(j * LANES, (j + 1) * LANES)
        values = (scores[:, cols] * factor).astype(jnp.bfloat16).astype(jnp.float32)
        occupancy = occupancy + values
        posterior.append(
            jnp.concatenate(
                [values, jnp.zeros((QPAD - rot_rows, LANES), jnp.float32)], axis=0
            ).astype(jnp.bfloat16)
        )
    posterior = jnp.concatenate(posterior, axis=1)
    weighted[:, : 2 * coefs] = lax.dot_general(
        posterior,
        shifted[...],
        (((1,), (0,)), ((), ())),
        preferred_element_type=jnp.float32,
    )[:rot_rows]
    occupancy = occupancy + pltpu.roll(occupancy, slots, 1)
    occupancy = jnp.where(lane_row < slots, occupancy, 0.0)
    occupancy = jnp.concatenate(
        [occupancy, jnp.zeros((QPAD - rot_rows, LANES), jnp.float32)], axis=0
    ).astype(jnp.bfloat16)
    weighted[:, 2 * coefs :] = (
        lax.dot_general(
            occupancy,
            jnp.concatenate([squares, squares], axis=0),
            (((1,), (0,)), ((), ())),
            preferred_element_type=jnp.float32,
        )[:rot_rows]
        / noise
    )

    def unrotate(firsts, j):
        sums = [jnp.zeros((8, LANES), jnp.float32) for _ in firsts]
        for p in range(pairs):
            lane = inverse[p, j]
            tile = inverse[p, tiles + j]
            found = [jnp.zeros((8, LANES), jnp.float32) for _ in firsts]
            for s in range(tiles):
                here = tile == s
                for i, first in enumerate(firsts):
                    base = first + s * LANES
                    picked = lane_take(weighted[p * 8 : (p + 1) * 8, base : base + LANES], lane)
                    found[i] = jnp.where(here, picked, found[i])
            sums = [x + y for x, y in zip(sums, found)]
        return [x + pltpu.roll(x, 4, 0) for x in sums]

    for w in range(tiles):
        (sums,) = unrotate([2 * coefs], w)
        piece_weight[2 * w] = jnp.where(low_half, pltpu.roll(sums, 64, 1), pltpu.roll(sums, 32, 1))
        piece_weight[2 * w + 1] = jnp.where(low_half, sums, pltpu.roll(sums, 96, 1))
    my_chip = lax.div(me_dp, 2)
    my_core = lax.rem(me_dp, 2)

    def pieces(j):
        for part, sums in enumerate(unrotate([0, coefs], j)):
            e = part * tiles + j
            data = jnp.where(low_half, sums, pltpu.roll(sums, 64, 1))
            both = jnp.where(lane_row < 64, data, piece_weight[e])
            piece_send[e, 0] = both[0:4]
            piece_send[e, 1] = both[4:8]

    def piece_start(e, core):
        target = 2 * e + core
        slot = lax.rem(target - me_dp + n_dp, n_dp) - 1
        pltpu.make_async_remote_copy(
            src_ref=piece_send.at[e, core],
            dst_ref=piece_recv.at[slot],
            send_sem=piece_sems.at[0],
            recv_sem=piece_sems.at[1],
            device_id=(target, me_cls),
            device_id_type=MESH,
        ).start()

    def chip_pieces(step, c):
        j = lax.rem(my_chip + 1 + step, tiles)
        pieces(j)
        for part in range(2):
            for core in range(2):
                piece_start(part * tiles + j, core)
        return c

    lax.fori_loop(0, tiles - 1, chip_pieces, 0)
    mine = lax.rem(my_chip, tiles)
    other = lax.rem(my_chip + tiles, 2 * tiles)
    pieces(mine)
    piece_start(other, 0)
    piece_start(other, 1)
    piece_start(my_chip, 1 - my_core)
    gathered = piece_send[my_chip, my_core]
    pltpu.make_async_copy(piece_recv, piece_recv, piece_sems.at[1]).wait()
    for o in range(n_dp - 1):
        gathered = gathered + piece_recv[o]
    data_ref[...] = gathered[:, :64]
    weight_ref[...] = pltpu.roll(gathered, 64, 1)[:, :32]
    pltpu.make_async_copy(piece_recv, piece_recv, piece_sems.at[0]).wait()


def body(particles, ctf, references, noise, rotations, counts):
    slots, coefs = ctf.shape
    classes = references.shape[0]
    n_dp = lax.axis_size("dp")
    n_cls = lax.axis_size("cls")
    padded = SHIFTS + 1
    trig = jnp.asarray(np.stack(phase_tables(coefs, padded), axis=1))
    rows = padded * slots
    pair_count = classes * TURNS
    vmem = pl.BlockSpec(memory_space=pltpu.VMEM)
    data, weight, evidence = pl.pallas_call(
        functools.partial(kernel, (n_dp, n_cls, slots, coefs)),
        out_shape=(
            jax.ShapeDtypeStruct((classes, 2 * coefs // n_dp), jnp.float32),
            jax.ShapeDtypeStruct((classes, coefs // n_dp), jnp.float32),
            jax.ShapeDtypeStruct((1, slots), jnp.float32),
        ),
        in_specs=[pl.BlockSpec(memory_space=pltpu.HBM)] * 7,
        out_specs=(vmem, vmem, vmem),
        scratch_shapes=[
            pltpu.SMEM(counts.shape, jnp.int32),
            pltpu.VMEM(particles.shape, jnp.float32),
            pltpu.VMEM(ctf.shape, jnp.float32),
            pltpu.VMEM(references.shape, references.dtype),
            pltpu.VMEM((1, coefs), jnp.float32),
            pltpu.VMEM(rotations.shape, jnp.int32),
            pltpu.VMEM(trig.shape, jnp.float32),
            pltpu.VMEM((slots, 2 * coefs), jnp.float32),
            pltpu.VMEM((slots, coefs), jnp.bfloat16),
            pltpu.VMEM((rows, 2 * coefs), jnp.bfloat16),
            pltpu.VMEM((pair_count, 2 * coefs), jnp.float32),
            pltpu.VMEM((pair_count, rows), jnp.float32),
            pltpu.VMEM((pair_count, 3 * coefs), jnp.float32),
            pltpu.VMEM((TURNS // 2, 2 * coefs // LANES, 8, LANES), jnp.int32),
            pltpu.VMEM((TURNS, 8, coefs), jnp.int32),
            pltpu.VMEM((8, 2 * coefs), jnp.float32),
            pltpu.VMEM((8, LANES), jnp.float32),
            pltpu.VMEM((n_cls - 1, 8, LANES), jnp.float32),
            pltpu.VMEM((n_dp // 2, 8, LANES), jnp.float32),
            pltpu.VMEM((n_dp // 2, 2, 4, LANES), jnp.float32),
            pltpu.VMEM((n_dp - 1, 4, LANES), jnp.float32),
            pltpu.SemaphoreType.DMA((7,)),
            pltpu.SemaphoreType.DMA((2,)),
            pltpu.SemaphoreType.DMA((2,)),
        ],
        compiler_params=pltpu.CompilerParams(
            collective_id=0, has_side_effects=True, vmem_limit_bytes=40 << 20
        ),
        name="class_average",
    )(
        *[
            pltpu.with_memory_space_constraint(x, pltpu.HBM)
            for x in (counts, particles, ctf, references, noise.reshape(1, coefs), rotations, trig)
        ]
    )
    return data, weight, evidence.reshape(slots)


def solution(mesh):
    placed = (P("dp", None), P("dp", None), P("cls", None), P(), P(), P("dp"))
    return jax.shard_map(
        body,
        mesh=mesh,
        in_specs=placed,
        out_specs=(P("cls", "dp"), P("cls", "dp"), P("dp")),
        check_vma=False,
    )
```

```python
import functools
import math

import jax
import jax.numpy as jnp
import numpy as np
from jax import lax
from jax.experimental import pallas as pl
from jax.experimental.pallas import tpu as pltpu
from jax.sharding import PartitionSpec as P

SIDE = 5
SHIFTS = 25
LANES = 128
TURNS = 18
QPAD = 80
MESH = pl.DeviceIdType.MESH


def phase_tables(coef_count):
    coefs = np.arange(coef_count)
    freq_x = (coefs % 32).astype(np.float32)
    freq_y = (coefs // 32 - coef_count // 64).astype(np.float32)
    offsets = np.arange(SHIFTS // 2)
    step_x = (offsets // SIDE - SIDE // 2).astype(np.float32)
    step_y = (offsets % SIDE - SIDE // 2).astype(np.float32)
    angles = np.float32(2.0 * math.pi / 64.0) * (
        step_x[:, None] * freq_x[None, :] + step_y[:, None] * freq_y[None, :]
    )
    wide = angles.astype(np.float32).astype(np.float64)
    return np.cos(wide).astype(np.float32), np.sin(wide).astype(np.float32)


def iota(shape, axis):
    return lax.broadcasted_iota(jnp.int32, shape, axis)


def lane_take(values, index):
    return jnp.take_along_axis(values, index, axis=1, mode="promise_in_bounds")


def kernel(
    dims,
    counts_hbm,
    part_hbm,
    ctf_hbm,
    refs_hbm,
    noise_hbm,
    rot_hbm,
    trig_hbm,
    data_ref,
    weight_ref,
    evid_ref,
    counts_ref,
    part_ref,
    ctf_ref,
    refs_ref,
    noise_ref,
    rot_ref,
    trig_ref,
    scaled,
    csq,
    shifted,
    rotated,
    scores,
    weighted,
    inverse,
    turns,
    total,
    stat_send,
    stat_recv,
    piece_weight,
    piece_send,
    piece_recv,
    load_sems,
    stat_sems,
    piece_sems,
):
    n_dp, n_cls, slots, coefs = dims
    tiles = coefs // LANES
    pairs = TURNS // 2
    shift_rows = shifted.shape[0]
    lanes_used = SHIFTS * slots
    me_dp = lax.axis_index("dp")
    me_cls = lax.axis_index("cls")
    my_chip = lax.div(me_dp, 2)
    my_core = lax.rem(me_dp, 2)

    loads = [
        pltpu.make_async_copy(source, target, load_sems.at[i])
        for i, (source, target) in enumerate(
            (
                (rot_hbm, rot_ref),
                (refs_hbm, refs_ref),
                (noise_hbm, noise_ref),
                (part_hbm, part_ref),
                (ctf_hbm, ctf_ref),
                (trig_hbm, trig_ref),
                (counts_hbm, counts_ref),
            )
        )
    ]
    for load in loads:
        load.start()

    barrier = pltpu.get_barrier_semaphore()

    def greet_dp(o, c):
        pl.semaphore_signal(
            barrier, inc=1, device_id=(lax.rem(me_dp + o, n_dp), me_cls), device_id_type=MESH
        )
        return c

    def greet_cls(o, c):
        pl.semaphore_signal(
            barrier, inc=1, device_id=(me_dp, lax.rem(me_cls + o, n_cls)), device_id_type=MESH
        )
        return c

    lax.fori_loop(1, n_dp, greet_dp, 0)
    lax.fori_loop(1, n_cls, greet_cls, 0)

    loads[0].wait()
    loads[1].wait()
    low_half = iota((8, LANES), 0) < 4
    for r in range(TURNS):
        turns[r] = jnp.broadcast_to(rot_ref[r : r + 1, :], (8, coefs))
    refs4 = refs_ref[...].astype(jnp.float32)
    total[...] = jnp.concatenate([refs4, refs4], axis=0)

    def rotate_pair(p, c):
        rows = pl.ds(pl.multiple_of(p * 8, 8), 8)
        for j in range(tiles):
            cols = slice(j * LANES, (j + 1) * LANES)
            index = jnp.where(low_half, turns[2 * p, :, cols], turns[2 * p + 1, :, cols])
            lane = index & (LANES - 1)
            tile = lax.shift_right_logical(index, 7)
            for part in range(2):
                found = jnp.zeros((8, LANES), jnp.float32)
                for s in range(tiles):
                    base = part * coefs + s * LANES
                    picked = lane_take(total[:, base : base + LANES], lane)
                    found = jnp.where(tile == s, picked, found)
                base = part * coefs + j * LANES
                rotated[rows, base : base + LANES] = found
        return c

    lax.fori_loop(0, pairs, rotate_pair, 0, unroll=3)
    for load in loads[2:]:
        load.wait()

    noise = noise_ref[...]
    transfer = ctf_ref[...]
    scaled[:, :coefs] = part_ref[:, :coefs] * transfer / noise
    scaled[:, coefs:] = part_ref[:, coefs:] * transfer / noise
    csq[...] = (transfer * transfer).astype(jnp.bfloat16)

    def shift_pair(s, c):
        cosine = trig_ref[s, 0:1, :]
        sine = trig_ref[s, 1:2, :]
        ahead = pl.ds(pl.multiple_of(s * slots, slots), slots)
        back = pl.ds(pl.multiple_of((SHIFTS - 1 - s) * slots, slots), slots)
        real = scaled[:, :coefs]
        imag = scaled[:, coefs:]
        real_cos = real * cosine
        imag_sin = imag * sine
        imag_cos = imag * cosine
        real_sin = real * sine
        shifted[ahead, :coefs] = (real_cos + imag_sin).astype(jnp.bfloat16)
        shifted[back, :coefs] = (real_cos - imag_sin).astype(jnp.bfloat16)
        shifted[ahead, coefs:] = (imag_cos - real_sin).astype(jnp.bfloat16)
        shifted[back, coefs:] = (imag_cos + real_sin).astype(jnp.bfloat16)
        return c

    lax.fori_loop(0, SHIFTS // 2, shift_pair, 0)
    shifted[SHIFTS // 2 * slots : (SHIFTS // 2 + 1) * slots, :] = scaled[...].astype(jnp.bfloat16)
    shifted[lanes_used:, :] = jnp.zeros((shift_rows - lanes_used, 2 * coefs), jnp.bfloat16)
    rot_rows = rotated.shape[0]
    turned = rotated[...]
    power = (
        (turned[:, :coefs] * turned[:, :coefs] + turned[:, coefs:] * turned[:, coefs:]) / noise
    ).astype(jnp.bfloat16)
    pad_rows = jnp.zeros((QPAD - rot_rows, 2 * coefs), jnp.float32)
    turned = jnp.concatenate([turned, pad_rows], axis=0).astype(jnp.bfloat16)
    squares = csq[...]
    contract_cols = (((1,), (1,)), ((), ()))
    penalty = lax.dot_general(
        power,
        jnp.concatenate([squares, squares], axis=0),
        contract_cols,
        preferred_element_type=jnp.float32,
    )
    half_penalty = 0.5 * penalty

    lane_row = iota((1, LANES), 1)
    peaks = jnp.full((8, LANES), -jnp.inf, jnp.float32)
    chunks = shift_rows // LANES
    cross_all = lax.dot_general(
        shifted[:shift_rows, :], turned, contract_cols, preferred_element_type=jnp.float32
    )
    for j in range(chunks):
        values = cross_all[j * LANES : (j + 1) * LANES, :].T[:rot_rows] - half_penalty
        if (j + 1) * LANES > lanes_used:
            values = jnp.where(j * LANES + lane_row < lanes_used, values, -1e30)
        scores[:, j * LANES : (j + 1) * LANES] = values
        for q in range(0, rot_rows, 8):
            peaks = jnp.maximum(peaks, values[q : q + 8])
    peak = jnp.max(peaks, axis=0, keepdims=True)
    peak = jnp.maximum(peak, pltpu.roll(peak, slots, 1))
    masses = jnp.zeros((8, LANES), jnp.float32)
    for j in range(chunks):
        cols = slice(j * LANES, (j + 1) * LANES)
        values = jnp.exp(scores[:, cols] - peak)
        if (j + 1) * LANES > lanes_used:
            values = jnp.where(j * LANES + lane_row < lanes_used, values, 0.0)
        scores[:, cols] = values
        for q in range(0, rot_rows, 8):
            masses = masses + values[q : q + 8]
    mass = jnp.sum(masses, axis=0, keepdims=True)
    mass = mass + pltpu.roll(mass, slots, 1)
    stat_send[...] = jnp.where(iota((8, LANES), 0) == 0, peak, mass)

    pl.semaphore_wait(barrier, n_dp - 1 + n_cls - 1)

    def stat_copy(o):
        return pltpu.make_async_remote_copy(
            src_ref=stat_send,
            dst_ref=stat_recv.at[o - 1],
            send_sem=stat_sems.at[0],
            recv_sem=stat_sems.at[1],
            device_id=(me_dp, lax.rem(me_cls + o, n_cls)),
            device_id_type=MESH,
        )

    def stat_start(o, c):
        stat_copy(o).start()
        return c

    lax.fori_loop(1, n_cls, stat_start, 0)

    place = iota((1, coefs), 1)
    place_low = (place & (LANES - 1)).astype(jnp.float32)
    place_high = lax.shift_right_logical(place, 7).astype(jnp.float32)

    def invert(r):
        row = turns[r, 0:1, :]
        lane = row & (LANES - 1)
        tile = lax.shift_right_logical(row, 7)
        hot = jnp.where(iota((LANES, coefs), 0) == lane, 1.0, 0.0).astype(jnp.bfloat16)
        mine = iota((tiles, coefs), 0) == tile
        source = jnp.concatenate(
            [jnp.where(mine, place_low, 0.0), jnp.where(mine, place_high, 0.0)], axis=0
        ).astype(jnp.bfloat16)
        return lax.dot_general(
            source, hot, contract_cols, preferred_element_type=jnp.float32
        ).astype(jnp.int32)

    def invert_pair(p, c):
        first = invert(2 * p)
        second = invert(2 * p + 1)
        for j in range(tiles):
            step = lax.rem(j + 2 * n_dp - my_chip - 1, tiles)
            for half in range(2):
                row = half * tiles + j
                inverse[p, half * tiles + step] = jnp.where(
                    low_half, first[row : row + 1], second[row : row + 1]
                )
        return c

    lax.fori_loop(0, pairs, invert_pair, 0, unroll=3)

    pltpu.make_async_copy(stat_recv, stat_recv, stat_sems.at[1]).wait()
    pltpu.make_async_copy(stat_recv, stat_recv, stat_sems.at[0]).wait()

    top = peak
    for o in range(n_cls - 1):
        top = jnp.maximum(top, stat_recv[o, 0:1, :])
    sums = mass * jnp.exp(peak - top)
    for o in range(n_cls - 1):
        sums = sums + stat_recv[o, 1:2, :] * jnp.exp(stat_recv[o, 0:1, :] - top)
    evidence = top + jnp.log(sums)
    live = (lane_row & (slots - 1)) < counts_ref[0] + counts_ref[1]
    factor = jnp.where(live, jnp.exp(peak - evidence), 0.0)
    evid_ref[...] = jnp.where(live, evidence, 0.0)[:, :slots]

    occupancy = jnp.zeros((rot_rows, LANES), jnp.float32)
    posterior = []
    for j in range(chunks):
        cols = slice(j * LANES, (j + 1) * LANES)
        values = (scores[:, cols] * factor).astype(jnp.bfloat16).astype(jnp.float32)
        occupancy = occupancy + values
        posterior.append(
            jnp.concatenate(
                [values, jnp.zeros((QPAD - rot_rows, LANES), jnp.float32)], axis=0
            ).astype(jnp.bfloat16)
        )
    posterior = jnp.concatenate(posterior, axis=1)
    weighted[:, : 2 * coefs] = lax.dot_general(
        posterior,
        shifted[...],
        (((1,), (0,)), ((), ())),
        preferred_element_type=jnp.float32,
    )[:rot_rows]
    occupancy = occupancy + pltpu.roll(occupancy, slots, 1)
    occupancy = jnp.where(lane_row < slots, occupancy, 0.0)
    occupancy = jnp.concatenate(
        [occupancy, jnp.zeros((QPAD - rot_rows, LANES), jnp.float32)], axis=0
    ).astype(jnp.bfloat16)
    weighted[:, 2 * coefs :] = (
        lax.dot_general(
            occupancy,
            jnp.concatenate([squares, squares], axis=0),
            (((1,), (0,)), ((), ())),
            preferred_element_type=jnp.float32,
        )[:rot_rows]
        / noise
    )

    def unrotate(firsts, step):
        sums = [jnp.zeros((8, LANES), jnp.float32) for _ in firsts]
        for p in range(pairs):
            lane = inverse[p, step]
            tile = inverse[p, tiles + step]
            found = [jnp.zeros((8, LANES), jnp.float32) for _ in firsts]
            for s in range(tiles):
                here = tile == s
                for i, first in enumerate(firsts):
                    base = first + s * LANES
                    picked = lane_take(weighted[p * 8 : (p + 1) * 8, base : base + LANES], lane)
                    found[i] = jnp.where(here, picked, found[i])
            sums = [x + y for x, y in zip(sums, found)]
        return [x + pltpu.roll(x, 4, 0) for x in sums]

    for step in range(tiles):
        w = lax.rem(my_chip + 1 + step, tiles)
        (sums,) = unrotate([2 * coefs], step)
        piece_weight[2 * w] = jnp.where(low_half, pltpu.roll(sums, 64, 1), pltpu.roll(sums, 32, 1))
        piece_weight[2 * w + 1] = jnp.where(low_half, sums, pltpu.roll(sums, 96, 1))

    def pieces(step):
        j = lax.rem(my_chip + 1 + step, tiles)
        for part, sums in enumerate(unrotate([0, coefs], step)):
            e = part * tiles + j
            data = jnp.where(low_half, sums, pltpu.roll(sums, 64, 1))
            both = jnp.where(lane_row < 64, data, piece_weight[e])
            piece_send[e, 0] = both[0:4]
            piece_send[e, 1] = both[4:8]

    def piece_start(e, core):
        target = 2 * e + core
        slot = lax.rem(target - me_dp + n_dp, n_dp) - 1
        pltpu.make_async_remote_copy(
            src_ref=piece_send.at[e, core],
            dst_ref=piece_recv.at[slot],
            send_sem=piece_sems.at[0],
            recv_sem=piece_sems.at[1],
            device_id=(target, me_cls),
            device_id_type=MESH,
        ).start()

    for step in range(tiles):
        pieces(step)
        j = lax.rem(my_chip + 1 + step, tiles)
        if step < tiles - 1:
            for part in range(2):
                for core in range(2):
                    piece_start(part * tiles + j, core)
    other = lax.rem(my_chip + tiles, 2 * tiles)
    piece_start(other, 0)
    piece_start(other, 1)
    piece_start(my_chip, 1 - my_core)
    gathered = piece_send[my_chip, my_core]
    pltpu.make_async_copy(piece_recv, piece_recv, piece_sems.at[1]).wait()
    for o in range(n_dp - 1):
        gathered = gathered + piece_recv[o]
    data_ref[...] = gathered[:, :64]
    weight_ref[...] = pltpu.roll(gathered, 64, 1)[:, :32]
    pltpu.make_async_copy(piece_recv, piece_recv, piece_sems.at[0]).wait()


def store(data, weight, evidence, data_out, weight_out, evidence_out, sems):
    copies = [
        pltpu.make_async_copy(data, data_out, sems.at[0]),
        pltpu.make_async_copy(weight, weight_out, sems.at[1]),
        pltpu.make_async_copy(evidence, evidence_out, sems.at[2]),
    ]
    for copy in copies:
        copy.start()
    for copy in copies:
        copy.wait()


def body(particles, ctf, references, noise, rotations, counts):
    slots, coefs = ctf.shape
    classes = references.shape[0]
    n_dp = lax.axis_size("dp")
    n_cls = lax.axis_size("cls")
    trig = jnp.asarray(np.stack(phase_tables(coefs), axis=1))
    rows = (SHIFTS + 1) * slots
    pair_count = classes * TURNS
    vmem = pl.BlockSpec(memory_space=pltpu.VMEM)
    data, weight, evidence = pl.pallas_call(
        functools.partial(kernel, (n_dp, n_cls, slots, coefs)),
        out_shape=(
            jax.ShapeDtypeStruct((classes, 2 * coefs // n_dp), jnp.float32),
            jax.ShapeDtypeStruct((classes, coefs // n_dp), jnp.float32),
            jax.ShapeDtypeStruct((1, slots), jnp.float32),
        ),
        in_specs=[pl.BlockSpec(memory_space=pltpu.HBM)] * 7,
        out_specs=(vmem, vmem, vmem),
        scratch_shapes=[
            pltpu.SMEM(counts.shape, jnp.int32),
            pltpu.VMEM(particles.shape, jnp.float32),
            pltpu.VMEM(ctf.shape, jnp.float32),
            pltpu.VMEM(references.shape, references.dtype),
            pltpu.VMEM((1, coefs), jnp.float32),
            pltpu.VMEM(rotations.shape, jnp.int32),
            pltpu.VMEM(trig.shape, jnp.float32),
            pltpu.VMEM((slots, 2 * coefs), jnp.float32),
            pltpu.VMEM((slots, coefs), jnp.bfloat16),
            pltpu.VMEM((rows, 2 * coefs), jnp.bfloat16),
            pltpu.VMEM((pair_count, 2 * coefs), jnp.float32),
            pltpu.VMEM((pair_count, rows), jnp.float32),
            pltpu.VMEM((pair_count, 3 * coefs), jnp.float32),
            pltpu.VMEM((TURNS // 2, 2 * coefs // LANES, 8, LANES), jnp.int32),
            pltpu.VMEM((TURNS, 8, coefs), jnp.int32),
            pltpu.VMEM((8, 2 * coefs), jnp.float32),
            pltpu.VMEM((8, LANES), jnp.float32),
            pltpu.VMEM((n_cls - 1, 8, LANES), jnp.float32),
            pltpu.VMEM((n_dp // 2, 8, LANES), jnp.float32),
            pltpu.VMEM((n_dp // 2, 2, 4, LANES), jnp.float32),
            pltpu.VMEM((n_dp - 1, 4, LANES), jnp.float32),
            pltpu.SemaphoreType.DMA((7,)),
            pltpu.SemaphoreType.DMA((2,)),
            pltpu.SemaphoreType.DMA((2,)),
        ],
        compiler_params=pltpu.CompilerParams(
            collective_id=0, has_side_effects=True, vmem_limit_bytes=40 << 20
        ),
        name="class_average",
    )(
        *[
            pltpu.with_memory_space_constraint(x, pltpu.HBM)
            for x in (counts, particles, ctf, references, noise.reshape(1, coefs), rotations, trig)
        ]
    )
    hbm = pl.BlockSpec(memory_space=pltpu.HBM)
    data, weight, evidence = pl.pallas_call(
        store,
        out_shape=tuple(jax.ShapeDtypeStruct(x.shape, x.dtype) for x in (data, weight, evidence)),
        in_specs=[vmem, vmem, vmem],
        out_specs=(hbm, hbm, hbm),
        scratch_shapes=[pltpu.SemaphoreType.DMA((3,))],
        name="store",
    )(*[pltpu.with_memory_space_constraint(x, pltpu.VMEM) for x in (data, weight, evidence)])
    return data, weight, evidence.reshape(slots)


def solution(mesh):
    placed = (P("dp", None), P("dp", None), P("cls", None), P(), P(), P("dp"))
    return jax.shard_map(
        body,
        mesh=mesh,
        in_specs=placed,
        out_specs=(P("cls", "dp"), P("cls", "dp"), P("dp")),
        check_vma=False,
    )
```

```python
import functools
import math

import jax
import jax.numpy as jnp
import numpy as np
from jax import lax
from jax.experimental import pallas as pl
from jax.experimental.pallas import tpu as pltpu
from jax.sharding import PartitionSpec as P

SIDE = 5
SHIFTS = 25
LANES = 128
TURNS = 18
QPAD = 80
MESH = pl.DeviceIdType.MESH


def phase_tables(coef_count):
    coefs = np.arange(coef_count)
    freq_x = (coefs % 32).astype(np.float32)
    freq_y = (coefs // 32 - coef_count // 64).astype(np.float32)
    offsets = np.arange(SHIFTS // 2)
    step_x = (offsets // SIDE - SIDE // 2).astype(np.float32)
    step_y = (offsets % SIDE - SIDE // 2).astype(np.float32)
    angles = np.float32(2.0 * math.pi / 64.0) * (
        step_x[:, None] * freq_x[None, :] + step_y[:, None] * freq_y[None, :]
    )
    wide = angles.astype(np.float32).astype(np.float64)
    return np.cos(wide).astype(np.float32), np.sin(wide).astype(np.float32)


def iota(shape, axis):
    return lax.broadcasted_iota(jnp.int32, shape, axis)


def lane_take(values, index):
    return jnp.take_along_axis(values, index, axis=1, mode="promise_in_bounds")


def kernel(
    dims,
    counts_hbm,
    part_hbm,
    ctf_hbm,
    refs_hbm,
    noise_hbm,
    rot_hbm,
    trig_hbm,
    data_ref,
    weight_ref,
    evid_ref,
    counts_ref,
    part_ref,
    ctf_ref,
    refs_ref,
    noise_ref,
    rot_ref,
    trig_ref,
    scaled,
    csq,
    shifted,
    rotated,
    scores,
    weighted,
    inverse,
    turns,
    total,
    stat_send,
    stat_recv,
    piece_weight,
    piece_send,
    piece_recv,
    load_sems,
    stat_sems,
    piece_sems,
):
    n_dp, n_cls, slots, coefs = dims
    tiles = coefs // LANES
    pairs = TURNS // 2
    shift_rows = shifted.shape[0]
    lanes_used = SHIFTS * slots
    me_dp = lax.axis_index("dp")
    me_cls = lax.axis_index("cls")
    my_chip = lax.div(me_dp, 2)
    my_core = lax.rem(me_dp, 2)

    loads = [
        pltpu.make_async_copy(source, target, load_sems.at[i])
        for i, (source, target) in enumerate(
            (
                (rot_hbm, rot_ref),
                (refs_hbm, refs_ref),
                (noise_hbm, noise_ref),
                (part_hbm, part_ref),
                (ctf_hbm, ctf_ref),
                (trig_hbm, trig_ref),
                (counts_hbm, counts_ref),
            )
        )
    ]
    for load in loads:
        load.start()

    barrier = pltpu.get_barrier_semaphore()

    def greet_dp(o, c):
        pl.semaphore_signal(
            barrier, inc=1, device_id=(lax.rem(me_dp + o, n_dp), me_cls), device_id_type=MESH
        )
        return c

    def greet_cls(o, c):
        pl.semaphore_signal(
            barrier, inc=1, device_id=(me_dp, lax.rem(me_cls + o, n_cls)), device_id_type=MESH
        )
        return c

    lax.fori_loop(1, n_dp, greet_dp, 0)
    lax.fori_loop(1, n_cls, greet_cls, 0)

    loads[0].wait()
    loads[1].wait()
    low_half = iota((8, LANES), 0) < 4
    for r in range(TURNS):
        turns[r] = jnp.broadcast_to(rot_ref[r : r + 1, :], (8, coefs))
    refs4 = refs_ref[...].astype(jnp.float32)
    total[...] = jnp.concatenate([refs4, refs4], axis=0)

    def rotate_pair(p, c):
        rows = pl.ds(pl.multiple_of(p * 8, 8), 8)
        for j in range(tiles):
            cols = slice(j * LANES, (j + 1) * LANES)
            index = jnp.where(low_half, turns[2 * p, :, cols], turns[2 * p + 1, :, cols])
            lane = index & (LANES - 1)
            tile = lax.shift_right_logical(index, 7)
            for part in range(2):
                found = jnp.zeros((8, LANES), jnp.float32)
                for s in range(tiles):
                    base = part * coefs + s * LANES
                    picked = lane_take(total[:, base : base + LANES], lane)
                    found = jnp.where(tile == s, picked, found)
                base = part * coefs + j * LANES
                rotated[rows, base : base + LANES] = found
        return c

    lax.fori_loop(0, pairs, rotate_pair, 0, unroll=3)
    for load in loads[2:]:
        load.wait()

    noise = noise_ref[...]
    transfer = ctf_ref[...]
    scaled[:, :coefs] = part_ref[:, :coefs] * transfer / noise
    scaled[:, coefs:] = part_ref[:, coefs:] * transfer / noise
    csq[...] = (transfer * transfer).astype(jnp.bfloat16)

    def shift_pair(s, c):
        cosine = trig_ref[s, 0:1, :]
        sine = trig_ref[s, 1:2, :]
        ahead = pl.ds(pl.multiple_of(s * slots, slots), slots)
        back = pl.ds(pl.multiple_of((SHIFTS - 1 - s) * slots, slots), slots)
        real = scaled[:, :coefs]
        imag = scaled[:, coefs:]
        real_cos = real * cosine
        imag_sin = imag * sine
        imag_cos = imag * cosine
        real_sin = real * sine
        shifted[ahead, :coefs] = (real_cos + imag_sin).astype(jnp.bfloat16)
        shifted[back, :coefs] = (real_cos - imag_sin).astype(jnp.bfloat16)
        shifted[ahead, coefs:] = (imag_cos - real_sin).astype(jnp.bfloat16)
        shifted[back, coefs:] = (imag_cos + real_sin).astype(jnp.bfloat16)
        return c

    lax.fori_loop(0, SHIFTS // 2, shift_pair, 0)
    shifted[SHIFTS // 2 * slots : (SHIFTS // 2 + 1) * slots, :] = scaled[...].astype(jnp.bfloat16)
    shifted[lanes_used:, :] = jnp.zeros((shift_rows - lanes_used, 2 * coefs), jnp.bfloat16)
    rot_rows = rotated.shape[0]
    turned = rotated[...]
    power = (
        (turned[:, :coefs] * turned[:, :coefs] + turned[:, coefs:] * turned[:, coefs:]) / noise
    ).astype(jnp.bfloat16)
    pad_rows = jnp.zeros((QPAD - rot_rows, 2 * coefs), jnp.float32)
    turned = jnp.concatenate([turned, pad_rows], axis=0).astype(jnp.bfloat16)
    squares = csq[...]
    contract_cols = (((1,), (1,)), ((), ()))
    penalty = lax.dot_general(
        power,
        jnp.concatenate([squares, squares], axis=0),
        contract_cols,
        preferred_element_type=jnp.float32,
    )
    half_penalty = 0.5 * penalty

    lane_row = iota((1, LANES), 1)
    peaks = jnp.full((8, LANES), -jnp.inf, jnp.float32)
    chunks = shift_rows // LANES
    cross_all = lax.dot_general(
        shifted[:shift_rows, :], turned, contract_cols, preferred_element_type=jnp.float32
    )
    for j in range(chunks):
        values = cross_all[j * LANES : (j + 1) * LANES, :].T[:rot_rows] - half_penalty
        if (j + 1) * LANES > lanes_used:
            values = jnp.where(j * LANES + lane_row < lanes_used, values, -1e30)
        scores[:, j * LANES : (j + 1) * LANES] = values
        for q in range(0, rot_rows, 8):
            peaks = jnp.maximum(peaks, values[q : q + 8])
    peak = jnp.max(peaks, axis=0, keepdims=True)
    peak = jnp.maximum(peak, pltpu.roll(peak, slots, 1))
    masses = jnp.zeros((8, LANES), jnp.float32)
    for j in range(chunks):
        cols = slice(j * LANES, (j + 1) * LANES)
        values = jnp.exp(scores[:, cols] - peak)
        if (j + 1) * LANES > lanes_used:
            values = jnp.where(j * LANES + lane_row < lanes_used, values, 0.0)
        scores[:, cols] = values
        for q in range(0, rot_rows, 8):
            masses = masses + values[q : q + 8]
    mass = jnp.sum(masses, axis=0, keepdims=True)
    mass = mass + pltpu.roll(mass, slots, 1)
    stat_send[...] = jnp.where(iota((8, LANES), 0) == 0, peak, mass)

    pl.semaphore_wait(barrier, n_dp - 1 + n_cls - 1)

    def stat_copy(o):
        return pltpu.make_async_remote_copy(
            src_ref=stat_send,
            dst_ref=stat_recv.at[o - 1],
            send_sem=stat_sems.at[0],
            recv_sem=stat_sems.at[1],
            device_id=(me_dp, lax.rem(me_cls + o, n_cls)),
            device_id_type=MESH,
        )

    def stat_start(o, c):
        stat_copy(o).start()
        return c

    lax.fori_loop(1, n_cls, stat_start, 0)

    place = iota((1, coefs), 1)
    place_low = (place & (LANES - 1)).astype(jnp.float32)
    place_high = lax.shift_right_logical(place, 7).astype(jnp.float32)

    def invert(r):
        row = turns[r, 0:1, :]
        lane = row & (LANES - 1)
        tile = lax.shift_right_logical(row, 7)
        hot = jnp.where(iota((LANES, coefs), 0) == lane, 1.0, 0.0).astype(jnp.bfloat16)
        mine = iota((tiles, coefs), 0) == tile
        source = jnp.concatenate(
            [jnp.where(mine, place_low, 0.0), jnp.where(mine, place_high, 0.0)], axis=0
        ).astype(jnp.bfloat16)
        return lax.dot_general(
            source, hot, contract_cols, preferred_element_type=jnp.float32
        ).astype(jnp.int32)

    def invert_pair(p, c):
        first = invert(2 * p)
        second = invert(2 * p + 1)
        for j in range(tiles):
            step = lax.rem(j + 2 * n_dp - my_chip - 1, tiles)
            for half in range(2):
                row = half * tiles + j
                inverse[p, half * tiles + step] = jnp.where(
                    low_half, first[row : row + 1], second[row : row + 1]
                )
        return c

    lax.fori_loop(0, pairs, invert_pair, 0, unroll=3)

    pltpu.make_async_copy(stat_recv, stat_recv, stat_sems.at[1]).wait()
    pltpu.make_async_copy(stat_recv, stat_recv, stat_sems.at[0]).wait()

    top = peak
    for o in range(n_cls - 1):
        top = jnp.maximum(top, stat_recv[o, 0:1, :])
    sums = mass * jnp.exp(peak - top)
    for o in range(n_cls - 1):
        sums = sums + stat_recv[o, 1:2, :] * jnp.exp(stat_recv[o, 0:1, :] - top)
    evidence = top + jnp.log(sums)
    live = (lane_row & (slots - 1)) < counts_ref[0] + counts_ref[1]
    factor = jnp.where(live, jnp.exp(peak - evidence), 0.0)
    evid_ref[...] = jnp.where(live, evidence, 0.0)[:, :slots]

    occupancy = jnp.zeros((rot_rows, LANES), jnp.float32)
    posterior = []
    for j in range(chunks):
        cols = slice(j * LANES, (j + 1) * LANES)
        values = (scores[:, cols] * factor).astype(jnp.bfloat16).astype(jnp.float32)
        occupancy = occupancy + values
        posterior.append(
            jnp.concatenate(
                [values, jnp.zeros((QPAD - rot_rows, LANES), jnp.float32)], axis=0
            ).astype(jnp.bfloat16)
        )
    occupancy = occupancy + pltpu.roll(occupancy, slots, 1)
    occupancy = jnp.where(lane_row < slots, occupancy, 0.0)
    occupancy = jnp.concatenate(
        [occupancy, jnp.zeros((QPAD - rot_rows, LANES), jnp.float32)], axis=0
    ).astype(jnp.bfloat16)
    weighted[:, 2 * coefs :] = (
        lax.dot_general(
            occupancy,
            jnp.concatenate([squares, squares], axis=0),
            (((1,), (0,)), ((), ())),
            preferred_element_type=jnp.float32,
        )[:rot_rows]
        / noise
    )

    def unrotate(firsts, step):
        sums = [jnp.zeros((8, LANES), jnp.float32) for _ in firsts]
        for p in range(pairs):
            lane = inverse[p, step]
            tile = inverse[p, tiles + step]
            found = [jnp.zeros((8, LANES), jnp.float32) for _ in firsts]
            for s in range(tiles):
                here = tile == s
                for i, first in enumerate(firsts):
                    base = first + s * LANES
                    picked = lane_take(weighted[p * 8 : (p + 1) * 8, base : base + LANES], lane)
                    found[i] = jnp.where(here, picked, found[i])
            sums = [x + y for x, y in zip(sums, found)]
        return [x + pltpu.roll(x, 4, 0) for x in sums]

    for step in range(tiles):
        w = lax.rem(my_chip + 1 + step, tiles)
        (sums,) = unrotate([2 * coefs], step)
        piece_weight[2 * w] = jnp.where(low_half, pltpu.roll(sums, 64, 1), pltpu.roll(sums, 32, 1))
        piece_weight[2 * w + 1] = jnp.where(low_half, sums, pltpu.roll(sums, 96, 1))

    posterior = jnp.concatenate(posterior, axis=1)
    weighted[:, : 2 * coefs] = lax.dot_general(
        posterior,
        shifted[...],
        (((1,), (0,)), ((), ())),
        preferred_element_type=jnp.float32,
    )[:rot_rows]
    def pieces(step):
        j = lax.rem(my_chip + 1 + step, tiles)
        for part, sums in enumerate(unrotate([0, coefs], step)):
            e = part * tiles + j
            data = jnp.where(low_half, sums, pltpu.roll(sums, 64, 1))
            both = jnp.where(lane_row < 64, data, piece_weight[e])
            piece_send[e, 0] = both[0:4]
            piece_send[e, 1] = both[4:8]

    def piece_start(e, core):
        target = 2 * e + core
        slot = lax.rem(target - me_dp + n_dp, n_dp) - 1
        pltpu.make_async_remote_copy(
            src_ref=piece_send.at[e, core],
            dst_ref=piece_recv.at[slot],
            send_sem=piece_sems.at[0],
            recv_sem=piece_sems.at[1],
            device_id=(target, me_cls),
            device_id_type=MESH,
        ).start()

    for step in range(tiles):
        pieces(step)
        j = lax.rem(my_chip + 1 + step, tiles)
        if step < tiles - 1:
            for part in range(2):
                for core in range(2):
                    piece_start(part * tiles + j, core)
    other = lax.rem(my_chip + tiles, 2 * tiles)
    piece_start(other, 0)
    piece_start(other, 1)
    piece_start(my_chip, 1 - my_core)
    gathered = piece_send[my_chip, my_core]
    pltpu.make_async_copy(piece_recv, piece_recv, piece_sems.at[1]).wait()
    for o in range(n_dp - 1):
        gathered = gathered + piece_recv[o]
    data_ref[...] = gathered[:, :64]
    weight_ref[...] = pltpu.roll(gathered, 64, 1)[:, :32]
    pltpu.make_async_copy(piece_recv, piece_recv, piece_sems.at[0]).wait()


def store(data, weight, evidence, data_out, weight_out, evidence_out, sems):
    copies = [
        pltpu.make_async_copy(data, data_out, sems.at[0]),
        pltpu.make_async_copy(weight, weight_out, sems.at[1]),
        pltpu.make_async_copy(evidence, evidence_out, sems.at[2]),
    ]
    for copy in copies:
        copy.start()
    for copy in copies:
        copy.wait()


def body(particles, ctf, references, noise, rotations, counts):
    slots, coefs = ctf.shape
    classes = references.shape[0]
    n_dp = lax.axis_size("dp")
    n_cls = lax.axis_size("cls")
    trig = jnp.asarray(np.stack(phase_tables(coefs), axis=1))
    rows = (SHIFTS + 1) * slots
    pair_count = classes * TURNS
    vmem = pl.BlockSpec(memory_space=pltpu.VMEM)
    data, weight, evidence = pl.pallas_call(
        functools.partial(kernel, (n_dp, n_cls, slots, coefs)),
        out_shape=(
            jax.ShapeDtypeStruct((classes, 2 * coefs // n_dp), jnp.float32),
            jax.ShapeDtypeStruct((classes, coefs // n_dp), jnp.float32),
            jax.ShapeDtypeStruct((1, slots), jnp.float32),
        ),
        in_specs=[pl.BlockSpec(memory_space=pltpu.HBM)] * 7,
        out_specs=(vmem, vmem, vmem),
        scratch_shapes=[
            pltpu.SMEM(counts.shape, jnp.int32),
            pltpu.VMEM(particles.shape, jnp.float32),
            pltpu.VMEM(ctf.shape, jnp.float32),
            pltpu.VMEM(references.shape, references.dtype),
            pltpu.VMEM((1, coefs), jnp.float32),
            pltpu.VMEM(rotations.shape, jnp.int32),
            pltpu.VMEM(trig.shape, jnp.float32),
            pltpu.VMEM((slots, 2 * coefs), jnp.float32),
            pltpu.VMEM((slots, coefs), jnp.bfloat16),
            pltpu.VMEM((rows, 2 * coefs), jnp.bfloat16),
            pltpu.VMEM((pair_count, 2 * coefs), jnp.float32),
            pltpu.VMEM((pair_count, rows), jnp.float32),
            pltpu.VMEM((pair_count, 3 * coefs), jnp.float32),
            pltpu.VMEM((TURNS // 2, 2 * coefs // LANES, 8, LANES), jnp.int32),
            pltpu.VMEM((TURNS, 8, coefs), jnp.int32),
            pltpu.VMEM((8, 2 * coefs), jnp.float32),
            pltpu.VMEM((8, LANES), jnp.float32),
            pltpu.VMEM((n_cls - 1, 8, LANES), jnp.float32),
            pltpu.VMEM((n_dp // 2, 8, LANES), jnp.float32),
            pltpu.VMEM((n_dp // 2, 2, 4, LANES), jnp.float32),
            pltpu.VMEM((n_dp - 1, 4, LANES), jnp.float32),
            pltpu.SemaphoreType.DMA((7,)),
            pltpu.SemaphoreType.DMA((2,)),
            pltpu.SemaphoreType.DMA((2,)),
        ],
        compiler_params=pltpu.CompilerParams(
            collective_id=0, has_side_effects=True, vmem_limit_bytes=40 << 20
        ),
        name="class_average",
    )(
        *[
            pltpu.with_memory_space_constraint(x, pltpu.HBM)
            for x in (counts, particles, ctf, references, noise.reshape(1, coefs), rotations, trig)
        ]
    )
    hbm = pl.BlockSpec(memory_space=pltpu.HBM)
    data, weight, evidence = pl.pallas_call(
        store,
        out_shape=tuple(jax.ShapeDtypeStruct(x.shape, x.dtype) for x in (data, weight, evidence)),
        in_specs=[vmem, vmem, vmem],
        out_specs=(hbm, hbm, hbm),
        scratch_shapes=[pltpu.SemaphoreType.DMA((3,))],
        name="store",
    )(*[pltpu.with_memory_space_constraint(x, pltpu.VMEM) for x in (data, weight, evidence)])
    return data, weight, evidence.reshape(slots)


def solution(mesh):
    placed = (P("dp", None), P("dp", None), P("cls", None), P(), P(), P("dp"))
    return jax.shard_map(
        body,
        mesh=mesh,
        in_specs=placed,
        out_specs=(P("cls", "dp"), P("cls", "dp"), P("dp")),
        check_vma=False,
    )
```

```python
import functools
import math

import jax
import jax.numpy as jnp
import numpy as np
from jax import lax
from jax.experimental import pallas as pl
from jax.experimental.pallas import tpu as pltpu
from jax.sharding import PartitionSpec as P

SIDE = 5
SHIFTS = 25
LANES = 128
TURNS = 18
QPAD = 80
MESH = pl.DeviceIdType.MESH


def phase_tables(coef_count):
    coefs = np.arange(coef_count)
    freq_x = (coefs % 32).astype(np.float32)
    freq_y = (coefs // 32 - coef_count // 64).astype(np.float32)
    offsets = np.arange(SHIFTS // 2)
    step_x = (offsets // SIDE - SIDE // 2).astype(np.float32)
    step_y = (offsets % SIDE - SIDE // 2).astype(np.float32)
    angles = np.float32(2.0 * math.pi / 64.0) * (
        step_x[:, None] * freq_x[None, :] + step_y[:, None] * freq_y[None, :]
    )
    wide = angles.astype(np.float32).astype(np.float64)
    return np.cos(wide).astype(np.float32), np.sin(wide).astype(np.float32)


def iota(shape, axis):
    return lax.broadcasted_iota(jnp.int32, shape, axis)


def lane_take(values, index):
    return jnp.take_along_axis(values, index, axis=1, mode="promise_in_bounds")


def kernel(
    dims,
    counts_hbm,
    part_hbm,
    ctf_hbm,
    refs_hbm,
    noise_hbm,
    rot_hbm,
    trig_hbm,
    data_ref,
    weight_ref,
    evid_ref,
    counts_ref,
    part_ref,
    ctf_ref,
    refs_ref,
    noise_ref,
    rot_ref,
    trig_ref,
    scaled,
    csq,
    shifted,
    rotated,
    scores,
    weighted,
    inverse,
    turns,
    total,
    stat_send,
    stat_recv,
    piece_weight,
    piece_send,
    piece_recv,
    load_sems,
    stat_sems,
    piece_sems,
):
    n_dp, n_cls, slots, coefs = dims
    tiles = coefs // LANES
    pairs = TURNS // 2
    shift_rows = shifted.shape[0]
    lanes_used = SHIFTS * slots
    me_dp = lax.axis_index("dp")
    me_cls = lax.axis_index("cls")
    my_chip = lax.div(me_dp, 2)
    my_core = lax.rem(me_dp, 2)

    loads = [
        pltpu.make_async_copy(source, target, load_sems.at[i])
        for i, (source, target) in enumerate(
            (
                (rot_hbm, rot_ref),
                (refs_hbm, refs_ref),
                (noise_hbm, noise_ref),
                (part_hbm, part_ref),
                (ctf_hbm, ctf_ref),
                (trig_hbm, trig_ref),
                (counts_hbm, counts_ref),
            )
        )
    ]
    for load in loads:
        load.start()

    barrier = pltpu.get_barrier_semaphore()

    def greet_dp(o, c):
        pl.semaphore_signal(
            barrier, inc=1, device_id=(lax.rem(me_dp + o, n_dp), me_cls), device_id_type=MESH
        )
        return c

    def greet_cls(o, c):
        pl.semaphore_signal(
            barrier, inc=1, device_id=(me_dp, lax.rem(me_cls + o, n_cls)), device_id_type=MESH
        )
        return c

    lax.fori_loop(1, n_dp, greet_dp, 0)
    lax.fori_loop(1, n_cls, greet_cls, 0)

    loads[0].wait()
    loads[1].wait()
    low_half = iota((8, LANES), 0) < 4
    for r in range(TURNS):
        turns[r] = jnp.broadcast_to(rot_ref[r : r + 1, :], (8, coefs))
    refs4 = refs_ref[...].astype(jnp.float32)
    total[...] = jnp.concatenate([refs4, refs4], axis=0)

    def rotate_pair(p, c):
        rows = pl.ds(pl.multiple_of(p * 8, 8), 8)
        for j in range(tiles):
            cols = slice(j * LANES, (j + 1) * LANES)
            index = jnp.where(low_half, turns[2 * p, :, cols], turns[2 * p + 1, :, cols])
            lane = index & (LANES - 1)
            tile = lax.shift_right_logical(index, 7)
            for part in range(2):
                found = jnp.zeros((8, LANES), jnp.float32)
                for s in range(tiles):
                    base = part * coefs + s * LANES
                    picked = lane_take(total[:, base : base + LANES], lane)
                    found = jnp.where(tile == s, picked, found)
                base = part * coefs + j * LANES
                rotated[rows, base : base + LANES] = found
        return c

    lax.fori_loop(0, pairs, rotate_pair, 0, unroll=3)
    for load in loads[2:]:
        load.wait()

    noise = noise_ref[...]
    transfer = ctf_ref[...]
    scaled[:, :coefs] = part_ref[:, :coefs] * transfer / noise
    scaled[:, coefs:] = part_ref[:, coefs:] * transfer / noise
    csq[...] = (transfer * transfer).astype(jnp.bfloat16)

    def shift_pair(s, c):
        cosine = trig_ref[s, 0:1, :]
        sine = trig_ref[s, 1:2, :]
        ahead = pl.ds(pl.multiple_of(s * slots, slots), slots)
        back = pl.ds(pl.multiple_of((SHIFTS - 1 - s) * slots, slots), slots)
        real = scaled[:, :coefs]
        imag = scaled[:, coefs:]
        real_cos = real * cosine
        imag_sin = imag * sine
        imag_cos = imag * cosine
        real_sin = real * sine
        shifted[ahead, :coefs] = (real_cos + imag_sin).astype(jnp.bfloat16)
        shifted[back, :coefs] = (real_cos - imag_sin).astype(jnp.bfloat16)
        shifted[ahead, coefs:] = (imag_cos - real_sin).astype(jnp.bfloat16)
        shifted[back, coefs:] = (imag_cos + real_sin).astype(jnp.bfloat16)
        return c

    lax.fori_loop(0, SHIFTS // 2, shift_pair, 0, unroll=2)
    shifted[SHIFTS // 2 * slots : (SHIFTS // 2 + 1) * slots, :] = scaled[...].astype(jnp.bfloat16)
    shifted[lanes_used:, :] = jnp.zeros((shift_rows - lanes_used, 2 * coefs), jnp.bfloat16)
    rot_rows = rotated.shape[0]
    turned = rotated[...]
    power = (
        (turned[:, :coefs] * turned[:, :coefs] + turned[:, coefs:] * turned[:, coefs:]) / noise
    ).astype(jnp.bfloat16)
    pad_rows = jnp.zeros((QPAD - rot_rows, 2 * coefs), jnp.float32)
    turned = jnp.concatenate([turned, pad_rows], axis=0).astype(jnp.bfloat16)
    squares = csq[...]
    contract_cols = (((1,), (1,)), ((), ()))
    penalty = lax.dot_general(
        power,
        jnp.concatenate([squares, squares], axis=0),
        contract_cols,
        preferred_element_type=jnp.float32,
    )
    half_penalty = 0.5 * penalty

    lane_row = iota((1, LANES), 1)
    peaks = jnp.full((8, LANES), -jnp.inf, jnp.float32)
    chunks = shift_rows // LANES
    cross_all = lax.dot_general(
        shifted[:shift_rows, :], turned, contract_cols, preferred_element_type=jnp.float32
    )
    for j in range(chunks):
        values = cross_all[j * LANES : (j + 1) * LANES, :].T[:rot_rows] - half_penalty
        if (j + 1) * LANES > lanes_used:
            values = jnp.where(j * LANES + lane_row < lanes_used, values, -1e30)
        scores[:, j * LANES : (j + 1) * LANES] = values
        for q in range(0, rot_rows, 8):
            peaks = jnp.maximum(peaks, values[q : q + 8])
    peak = jnp.max(peaks, axis=0, keepdims=True)
    peak = jnp.maximum(peak, pltpu.roll(peak, slots, 1))
    masses = jnp.zeros((8, LANES), jnp.float32)
    for j in range(chunks):
        cols = slice(j * LANES, (j + 1) * LANES)
        values = jnp.exp(scores[:, cols] - peak)
        if (j + 1) * LANES > lanes_used:
            values = jnp.where(j * LANES + lane_row < lanes_used, values, 0.0)
        scores[:, cols] = values
        for q in range(0, rot_rows, 8):
            masses = masses + values[q : q + 8]
    mass = jnp.sum(masses, axis=0, keepdims=True)
    mass = mass + pltpu.roll(mass, slots, 1)
    stat_send[...] = jnp.where(iota((8, LANES), 0) == 0, peak, mass)

    pl.semaphore_wait(barrier, n_dp - 1 + n_cls - 1)

    def stat_copy(o):
        return pltpu.make_async_remote_copy(
            src_ref=stat_send,
            dst_ref=stat_recv.at[o - 1],
            send_sem=stat_sems.at[0],
            recv_sem=stat_sems.at[1],
            device_id=(me_dp, lax.rem(me_cls + o, n_cls)),
            device_id_type=MESH,
        )

    def stat_start(o, c):
        stat_copy(o).start()
        return c

    lax.fori_loop(1, n_cls, stat_start, 0)

    place = iota((1, coefs), 1)
    place_low = (place & (LANES - 1)).astype(jnp.float32)
    place_high = lax.shift_right_logical(place, 7).astype(jnp.float32)

    def invert(r):
        row = turns[r, 0:1, :]
        lane = row & (LANES - 1)
        tile = lax.shift_right_logical(row, 7)
        hot = jnp.where(iota((LANES, coefs), 0) == lane, 1.0, 0.0).astype(jnp.bfloat16)
        mine = iota((tiles, coefs), 0) == tile
        source = jnp.concatenate(
            [jnp.where(mine, place_low, 0.0), jnp.where(mine, place_high, 0.0)], axis=0
        ).astype(jnp.bfloat16)
        return lax.dot_general(
            source, hot, contract_cols, preferred_element_type=jnp.float32
        ).astype(jnp.int32)

    def invert_pair(p, c):
        first = invert(2 * p)
        second = invert(2 * p + 1)
        for j in range(tiles):
            step = lax.rem(j + 2 * n_dp - my_chip - 1, tiles)
            for half in range(2):
                row = half * tiles + j
                inverse[p, half * tiles + step] = jnp.where(
                    low_half, first[row : row + 1], second[row : row + 1]
                )
        return c

    lax.fori_loop(0, pairs, invert_pair, 0, unroll=3)

    pltpu.make_async_copy(stat_recv, stat_recv, stat_sems.at[1]).wait()
    pltpu.make_async_copy(stat_recv, stat_recv, stat_sems.at[0]).wait()

    top = peak
    for o in range(n_cls - 1):
        top = jnp.maximum(top, stat_recv[o, 0:1, :])
    sums = mass * jnp.exp(peak - top)
    for o in range(n_cls - 1):
        sums = sums + stat_recv[o, 1:2, :] * jnp.exp(stat_recv[o, 0:1, :] - top)
    evidence = top + jnp.log(sums)
    live = (lane_row & (slots - 1)) < counts_ref[0] + counts_ref[1]
    factor = jnp.where(live, jnp.exp(peak - evidence), 0.0)
    evid_ref[...] = jnp.where(live, evidence, 0.0)[:, :slots]

    occupancy = jnp.zeros((rot_rows, LANES), jnp.float32)
    posterior = []
    for j in range(chunks):
        cols = slice(j * LANES, (j + 1) * LANES)
        values = (scores[:, cols] * factor).astype(jnp.bfloat16).astype(jnp.float32)
        occupancy = occupancy + values
        posterior.append(
            jnp.concatenate(
                [values, jnp.zeros((QPAD - rot_rows, LANES), jnp.float32)], axis=0
            ).astype(jnp.bfloat16)
        )
    occupancy = occupancy + pltpu.roll(occupancy, slots, 1)
    occupancy = jnp.where(lane_row < slots, occupancy, 0.0)
    occupancy = jnp.concatenate(
        [occupancy, jnp.zeros((QPAD - rot_rows, LANES), jnp.float32)], axis=0
    ).astype(jnp.bfloat16)
    weighted[:, 2 * coefs :] = (
        lax.dot_general(
            occupancy,
            jnp.concatenate([squares, squares], axis=0),
            (((1,), (0,)), ((), ())),
            preferred_element_type=jnp.float32,
        )[:rot_rows]
        / noise
    )

    def unrotate(firsts, step):
        sums = [jnp.zeros((8, LANES), jnp.float32) for _ in firsts]
        for p in range(pairs):
            lane = inverse[p, step]
            tile = inverse[p, tiles + step]
            found = [jnp.zeros((8, LANES), jnp.float32) for _ in firsts]
            for s in range(tiles):
                here = tile == s
                for i, first in enumerate(firsts):
                    base = first + s * LANES
                    picked = lane_take(weighted[p * 8 : (p + 1) * 8, base : base + LANES], lane)
                    found[i] = jnp.where(here, picked, found[i])
            sums = [x + y for x, y in zip(sums, found)]
        return [x + pltpu.roll(x, 4, 0) for x in sums]

    for step in range(tiles):
        w = lax.rem(my_chip + 1 + step, tiles)
        (sums,) = unrotate([2 * coefs], step)
        piece_weight[2 * w] = jnp.where(low_half, pltpu.roll(sums, 64, 1), pltpu.roll(sums, 32, 1))
        piece_weight[2 * w + 1] = jnp.where(low_half, sums, pltpu.roll(sums, 96, 1))

    posterior = jnp.concatenate(posterior, axis=1)
    weighted[:, : 2 * coefs] = lax.dot_general(
        posterior,
        shifted[...],
        (((1,), (0,)), ((), ())),
        preferred_element_type=jnp.float32,
    )[:rot_rows]
    def pieces(step):
        j = lax.rem(my_chip + 1 + step, tiles)
        for part, sums in enumerate(unrotate([0, coefs], step)):
            e = part * tiles + j
            data = jnp.where(low_half, sums, pltpu.roll(sums, 64, 1))
            both = jnp.where(lane_row < 64, data, piece_weight[e])
            piece_send[e, 0] = both[0:4]
            piece_send[e, 1] = both[4:8]

    def piece_start(e, core):
        target = 2 * e + core
        slot = lax.rem(target - me_dp + n_dp, n_dp) - 1
        pltpu.make_async_remote_copy(
            src_ref=piece_send.at[e, core],
            dst_ref=piece_recv.at[slot],
            send_sem=piece_sems.at[0],
            recv_sem=piece_sems.at[1],
            device_id=(target, me_cls),
            device_id_type=MESH,
        ).start()

    for step in range(tiles):
        pieces(step)
        j = lax.rem(my_chip + 1 + step, tiles)
        if step < tiles - 1:
            for part in range(2):
                for core in range(2):
                    piece_start(part * tiles + j, core)
    other = lax.rem(my_chip + tiles, 2 * tiles)
    piece_start(other, 0)
    piece_start(other, 1)
    piece_start(my_chip, 1 - my_core)
    gathered = piece_send[my_chip, my_core]
    pltpu.make_async_copy(piece_recv, piece_recv, piece_sems.at[1]).wait()
    for o in range(n_dp - 1):
        gathered = gathered + piece_recv[o]
    data_ref[...] = gathered[:, :64]
    weight_ref[...] = pltpu.roll(gathered, 64, 1)[:, :32]
    pltpu.make_async_copy(piece_recv, piece_recv, piece_sems.at[0]).wait()


def store(data, weight, evidence, data_out, weight_out, evidence_out, sems):
    copies = [
        pltpu.make_async_copy(data, data_out, sems.at[0]),
        pltpu.make_async_copy(weight, weight_out, sems.at[1]),
        pltpu.make_async_copy(evidence, evidence_out, sems.at[2]),
    ]
    for copy in copies:
        copy.start()
    for copy in copies:
        copy.wait()


def body(particles, ctf, references, noise, rotations, counts):
    slots, coefs = ctf.shape
    classes = references.shape[0]
    n_dp = lax.axis_size("dp")
    n_cls = lax.axis_size("cls")
    trig = jnp.asarray(np.stack(phase_tables(coefs), axis=1))
    rows = (SHIFTS + 1) * slots
    pair_count = classes * TURNS
    vmem = pl.BlockSpec(memory_space=pltpu.VMEM)
    data, weight, evidence = pl.pallas_call(
        functools.partial(kernel, (n_dp, n_cls, slots, coefs)),
        out_shape=(
            jax.ShapeDtypeStruct((classes, 2 * coefs // n_dp), jnp.float32),
            jax.ShapeDtypeStruct((classes, coefs // n_dp), jnp.float32),
            jax.ShapeDtypeStruct((1, slots), jnp.float32),
        ),
        in_specs=[pl.BlockSpec(memory_space=pltpu.HBM)] * 7,
        out_specs=(vmem, vmem, vmem),
        scratch_shapes=[
            pltpu.SMEM(counts.shape, jnp.int32),
            pltpu.VMEM(particles.shape, jnp.float32),
            pltpu.VMEM(ctf.shape, jnp.float32),
            pltpu.VMEM(references.shape, references.dtype),
            pltpu.VMEM((1, coefs), jnp.float32),
            pltpu.VMEM(rotations.shape, jnp.int32),
            pltpu.VMEM(trig.shape, jnp.float32),
            pltpu.VMEM((slots, 2 * coefs), jnp.float32),
            pltpu.VMEM((slots, coefs), jnp.bfloat16),
            pltpu.VMEM((rows, 2 * coefs), jnp.bfloat16),
            pltpu.VMEM((pair_count, 2 * coefs), jnp.float32),
            pltpu.VMEM((pair_count, rows), jnp.float32),
            pltpu.VMEM((pair_count, 3 * coefs), jnp.float32),
            pltpu.VMEM((TURNS // 2, 2 * coefs // LANES, 8, LANES), jnp.int32),
            pltpu.VMEM((TURNS, 8, coefs), jnp.int32),
            pltpu.VMEM((8, 2 * coefs), jnp.float32),
            pltpu.VMEM((8, LANES), jnp.float32),
            pltpu.VMEM((n_cls - 1, 8, LANES), jnp.float32),
            pltpu.VMEM((n_dp // 2, 8, LANES), jnp.float32),
            pltpu.VMEM((n_dp // 2, 2, 4, LANES), jnp.float32),
            pltpu.VMEM((n_dp - 1, 4, LANES), jnp.float32),
            pltpu.SemaphoreType.DMA((7,)),
            pltpu.SemaphoreType.DMA((2,)),
            pltpu.SemaphoreType.DMA((2,)),
        ],
        compiler_params=pltpu.CompilerParams(
            collective_id=0, has_side_effects=True, vmem_limit_bytes=40 << 20
        ),
        name="class_average",
    )(
        *[
            pltpu.with_memory_space_constraint(x, pltpu.HBM)
            for x in (counts, particles, ctf, references, noise.reshape(1, coefs), rotations, trig)
        ]
    )
    hbm = pl.BlockSpec(memory_space=pltpu.HBM)
    data, weight, evidence = pl.pallas_call(
        store,
        out_shape=tuple(jax.ShapeDtypeStruct(x.shape, x.dtype) for x in (data, weight, evidence)),
        in_specs=[vmem, vmem, vmem],
        out_specs=(hbm, hbm, hbm),
        scratch_shapes=[pltpu.SemaphoreType.DMA((3,))],
        name="store",
    )(*[pltpu.with_memory_space_constraint(x, pltpu.VMEM) for x in (data, weight, evidence)])
    return data, weight, evidence.reshape(slots)


def solution(mesh):
    placed = (P("dp", None), P("dp", None), P("cls", None), P(), P(), P("dp"))
    return jax.shard_map(
        body,
        mesh=mesh,
        in_specs=placed,
        out_specs=(P("cls", "dp"), P("cls", "dp"), P("dp")),
        check_vma=False,
    )
```

```python
import functools
import math

import jax
import jax.numpy as jnp
import numpy as np
from jax import lax
from jax.experimental import pallas as pl
from jax.experimental.pallas import tpu as pltpu
from jax.sharding import PartitionSpec as P

SIDE = 5
SHIFTS = 25
LANES = 128
TURNS = 18
QPAD = 80
MESH = pl.DeviceIdType.MESH


def phase_tables(coef_count):
    coefs = np.arange(coef_count)
    freq_x = (coefs % 32).astype(np.float32)
    freq_y = (coefs // 32 - coef_count // 64).astype(np.float32)
    offsets = np.arange(SHIFTS // 2)
    step_x = (offsets // SIDE - SIDE // 2).astype(np.float32)
    step_y = (offsets % SIDE - SIDE // 2).astype(np.float32)
    angles = np.float32(2.0 * math.pi / 64.0) * (
        step_x[:, None] * freq_x[None, :] + step_y[:, None] * freq_y[None, :]
    )
    wide = angles.astype(np.float32).astype(np.float64)
    return np.cos(wide).astype(np.float32), np.sin(wide).astype(np.float32)


def iota(shape, axis):
    return lax.broadcasted_iota(jnp.int32, shape, axis)


def lane_take(values, index):
    return jnp.take_along_axis(values, index, axis=1, mode="promise_in_bounds")


def kernel(
    dims,
    counts_hbm,
    part_hbm,
    ctf_hbm,
    refs_hbm,
    noise_hbm,
    rot_hbm,
    trig_hbm,
    data_ref,
    weight_ref,
    evid_ref,
    counts_ref,
    part_ref,
    ctf_ref,
    refs_ref,
    noise_ref,
    rot_ref,
    trig_ref,
    scaled,
    csq,
    shifted,
    rotated,
    scores,
    weighted,
    inverse,
    turns,
    total,
    stat_send,
    stat_recv,
    piece_weight,
    piece_send,
    piece_recv,
    load_sems,
    stat_sems,
    piece_sems,
):
    n_dp, n_cls, slots, coefs = dims
    tiles = coefs // LANES
    pairs = TURNS // 2
    shift_rows = shifted.shape[0]
    lanes_used = SHIFTS * slots
    me_dp = lax.axis_index("dp")
    me_cls = lax.axis_index("cls")
    my_chip = lax.div(me_dp, 2)
    my_core = lax.rem(me_dp, 2)

    loads = [
        pltpu.make_async_copy(source, target, load_sems.at[i])
        for i, (source, target) in enumerate(
            (
                (rot_hbm, rot_ref),
                (refs_hbm, refs_ref),
                (noise_hbm, noise_ref),
                (part_hbm, part_ref),
                (ctf_hbm, ctf_ref),
                (trig_hbm, trig_ref),
                (counts_hbm, counts_ref),
            )
        )
    ]
    for load in loads:
        load.start()

    barrier = pltpu.get_barrier_semaphore()

    def greet_dp(o, c):
        pl.semaphore_signal(
            barrier, inc=1, device_id=(lax.rem(me_dp + o, n_dp), me_cls), device_id_type=MESH
        )
        return c

    def greet_cls(o, c):
        pl.semaphore_signal(
            barrier, inc=1, device_id=(me_dp, lax.rem(me_cls + o, n_cls)), device_id_type=MESH
        )
        return c

    lax.fori_loop(1, n_dp, greet_dp, 0)
    lax.fori_loop(1, n_cls, greet_cls, 0)

    loads[0].wait()
    loads[1].wait()
    low_half = iota((8, LANES), 0) < 4
    for r in range(TURNS):
        turns[r] = jnp.broadcast_to(rot_ref[r : r + 1, :], (8, coefs))
    refs4 = refs_ref[...].astype(jnp.float32)
    total[...] = jnp.concatenate([refs4, refs4], axis=0)

    def rotate_pair(p, c):
        rows = pl.ds(pl.multiple_of(p * 8, 8), 8)
        for j in range(tiles):
            cols = slice(j * LANES, (j + 1) * LANES)
            index = jnp.where(low_half, turns[2 * p, :, cols], turns[2 * p + 1, :, cols])
            lane = index & (LANES - 1)
            tile = lax.shift_right_logical(index, 7)
            for part in range(2):
                found = jnp.zeros((8, LANES), jnp.float32)
                for s in range(tiles):
                    base = part * coefs + s * LANES
                    picked = lane_take(total[:, base : base + LANES], lane)
                    found = jnp.where(tile == s, picked, found)
                base = part * coefs + j * LANES
                rotated[rows, base : base + LANES] = found
        return c

    lax.fori_loop(0, pairs, rotate_pair, 0, unroll=3)
    for load in loads[2:]:
        load.wait()

    noise = noise_ref[...]
    transfer = ctf_ref[...]
    scaled[:, :coefs] = part_ref[:, :coefs] * transfer / noise
    scaled[:, coefs:] = part_ref[:, coefs:] * transfer / noise
    csq[...] = (transfer * transfer).astype(jnp.bfloat16)

    def shift_pair(s, c):
        cosine = trig_ref[s, 0:1, :]
        sine = trig_ref[s, 1:2, :]
        ahead = pl.ds(pl.multiple_of(s * slots, slots), slots)
        back = pl.ds(pl.multiple_of((SHIFTS - 1 - s) * slots, slots), slots)
        real = scaled[:, :coefs]
        imag = scaled[:, coefs:]
        real_cos = real * cosine
        imag_sin = imag * sine
        imag_cos = imag * cosine
        real_sin = real * sine
        shifted[ahead, :coefs] = (real_cos + imag_sin).astype(jnp.bfloat16)
        shifted[back, :coefs] = (real_cos - imag_sin).astype(jnp.bfloat16)
        shifted[ahead, coefs:] = (imag_cos - real_sin).astype(jnp.bfloat16)
        shifted[back, coefs:] = (imag_cos + real_sin).astype(jnp.bfloat16)
        return c

    lax.fori_loop(0, SHIFTS // 2, shift_pair, 0)
    shifted[SHIFTS // 2 * slots : (SHIFTS // 2 + 1) * slots, :] = scaled[...].astype(jnp.bfloat16)
    shifted[lanes_used:, :] = jnp.zeros((shift_rows - lanes_used, 2 * coefs), jnp.bfloat16)
    rot_rows = rotated.shape[0]
    turned = rotated[...]
    power = (
        (turned[:, :coefs] * turned[:, :coefs] + turned[:, coefs:] * turned[:, coefs:]) / noise
    ).astype(jnp.bfloat16)
    pad_rows = jnp.zeros((QPAD - rot_rows, 2 * coefs), jnp.float32)
    turned = jnp.concatenate([turned, pad_rows], axis=0).astype(jnp.bfloat16)
    squares = csq[...]
    contract_cols = (((1,), (1,)), ((), ()))
    penalty = lax.dot_general(
        power,
        jnp.concatenate([squares, squares], axis=0),
        contract_cols,
        preferred_element_type=jnp.float32,
    )
    half_penalty = 0.5 * penalty

    lane_row = iota((1, LANES), 1)
    peaks = jnp.full((8, LANES), -jnp.inf, jnp.float32)
    chunks = shift_rows // LANES
    cross_all = lax.dot_general(
        shifted[:shift_rows, :], turned, contract_cols, preferred_element_type=jnp.float32
    )
    for j in range(chunks):
        values = cross_all[j * LANES : (j + 1) * LANES, :].T[:rot_rows] - half_penalty
        if (j + 1) * LANES > lanes_used:
            values = jnp.where(j * LANES + lane_row < lanes_used, values, -1e30)
        scores[:, j * LANES : (j + 1) * LANES] = values
        for q in range(0, rot_rows, 8):
            peaks = jnp.maximum(peaks, values[q : q + 8])
    peak = jnp.max(peaks, axis=0, keepdims=True)
    peak = jnp.maximum(peak, pltpu.roll(peak, slots, 1))
    masses = jnp.zeros((8, LANES), jnp.float32)
    for j in range(chunks):
        cols = slice(j * LANES, (j + 1) * LANES)
        values = jnp.exp(scores[:, cols] - peak)
        if (j + 1) * LANES > lanes_used:
            values = jnp.where(j * LANES + lane_row < lanes_used, values, 0.0)
        scores[:, cols] = values
        for q in range(0, rot_rows, 8):
            masses = masses + values[q : q + 8]
    mass = jnp.sum(masses, axis=0, keepdims=True)
    mass = mass + pltpu.roll(mass, slots, 1)
    stat_send[...] = jnp.where(iota((8, LANES), 0) == 0, peak, mass)

    pl.semaphore_wait(barrier, n_dp - 1 + n_cls - 1)

    def stat_copy(o):
        return pltpu.make_async_remote_copy(
            src_ref=stat_send,
            dst_ref=stat_recv.at[o - 1],
            send_sem=stat_sems.at[0],
            recv_sem=stat_sems.at[1],
            device_id=(me_dp, lax.rem(me_cls + o, n_cls)),
            device_id_type=MESH,
        )

    def stat_start(o, c):
        stat_copy(o).start()
        return c

    lax.fori_loop(1, n_cls, stat_start, 0)

    place = iota((1, coefs), 1)
    place_low = (place & (LANES - 1)).astype(jnp.float32)
    place_high = lax.shift_right_logical(place, 7).astype(jnp.float32)

    def invert(r):
        row = turns[r, 0:1, :]
        lane = row & (LANES - 1)
        tile = lax.shift_right_logical(row, 7)
        hot = jnp.where(iota((LANES, coefs), 0) == lane, 1.0, 0.0).astype(jnp.bfloat16)
        mine = iota((tiles, coefs), 0) == tile
        source = jnp.concatenate(
            [jnp.where(mine, place_low, 0.0), jnp.where(mine, place_high, 0.0)], axis=0
        ).astype(jnp.bfloat16)
        return lax.dot_general(
            source, hot, contract_cols, preferred_element_type=jnp.float32
        ).astype(jnp.int32)

    def invert_pair(p, c):
        first = invert(2 * p)
        second = invert(2 * p + 1)
        for j in range(tiles):
            step = lax.rem(j + 2 * n_dp - my_chip - 1, tiles)
            for half in range(2):
                row = half * tiles + j
                inverse[p, half * tiles + step] = jnp.where(
                    low_half, first[row : row + 1], second[row : row + 1]
                )
        return c

    lax.fori_loop(0, pairs, invert_pair, 0, unroll=3)

    pltpu.make_async_copy(stat_recv, stat_recv, stat_sems.at[1]).wait()
    pltpu.make_async_copy(stat_recv, stat_recv, stat_sems.at[0]).wait()

    top = peak
    for o in range(n_cls - 1):
        top = jnp.maximum(top, stat_recv[o, 0:1, :])
    sums = mass * jnp.exp(peak - top)
    for o in range(n_cls - 1):
        sums = sums + stat_recv[o, 1:2, :] * jnp.exp(stat_recv[o, 0:1, :] - top)
    evidence = top + jnp.log(sums)
    live = (lane_row & (slots - 1)) < counts_ref[0] + counts_ref[1]
    factor = jnp.where(live, jnp.exp(peak - evidence), 0.0)
    evid_ref[...] = jnp.where(live, evidence, 0.0)[:, :slots]

    occupancy = jnp.zeros((rot_rows, LANES), jnp.float32)
    posterior = []
    for j in range(chunks):
        cols = slice(j * LANES, (j + 1) * LANES)
        values = (scores[:, cols] * factor).astype(jnp.bfloat16).astype(jnp.float32)
        occupancy = occupancy + values
        posterior.append(
            jnp.concatenate(
                [values, jnp.zeros((QPAD - rot_rows, LANES), jnp.float32)], axis=0
            ).astype(jnp.bfloat16)
        )
    occupancy = occupancy + pltpu.roll(occupancy, slots, 1)
    occupancy = jnp.where(lane_row < slots, occupancy, 0.0)
    occupancy = jnp.concatenate(
        [occupancy, jnp.zeros((QPAD - rot_rows, LANES), jnp.float32)], axis=0
    ).astype(jnp.bfloat16)
    weighted[:, 2 * coefs :] = (
        lax.dot_general(
            occupancy,
            jnp.concatenate([squares, squares], axis=0),
            (((1,), (0,)), ((), ())),
            preferred_element_type=jnp.float32,
        )[:rot_rows]
        / noise
    )

    def unrotate(firsts, step):
        sums = [jnp.zeros((8, LANES), jnp.float32) for _ in firsts]
        for p in range(pairs):
            lane = inverse[p, step]
            tile = inverse[p, tiles + step]
            found = [jnp.zeros((8, LANES), jnp.float32) for _ in firsts]
            for s in range(tiles):
                here = tile == s
                for i, first in enumerate(firsts):
                    base = first + s * LANES
                    picked = lane_take(weighted[p * 8 : (p + 1) * 8, base : base + LANES], lane)
                    found[i] = jnp.where(here, picked, found[i])
            sums = [x + y for x, y in zip(sums, found)]
        return [x + pltpu.roll(x, 4, 0) for x in sums]

    for step in range(tiles):
        w = lax.rem(my_chip + 1 + step, tiles)
        (sums,) = unrotate([2 * coefs], step)
        piece_weight[2 * w] = jnp.where(low_half, pltpu.roll(sums, 64, 1), pltpu.roll(sums, 32, 1))
        piece_weight[2 * w + 1] = jnp.where(low_half, sums, pltpu.roll(sums, 96, 1))

    posterior = jnp.concatenate(posterior, axis=1)
    weighted[:, : 2 * coefs] = lax.dot_general(
        posterior,
        shifted[...],
        (((1,), (0,)), ((), ())),
        preferred_element_type=jnp.float32,
    )[:rot_rows]
    def pieces(step):
        j = lax.rem(my_chip + 1 + step, tiles)
        for part, sums in enumerate(unrotate([0, coefs], step)):
            e = part * tiles + j
            data = jnp.where(low_half, sums, pltpu.roll(sums, 64, 1))
            both = jnp.where(lane_row < 64, data, piece_weight[e])
            piece_send[e, 0] = both[0:4]
            piece_send[e, 1] = both[4:8]

    def piece_start(e, core):
        target = 2 * e + core
        slot = lax.rem(target - me_dp + n_dp, n_dp) - 1
        pltpu.make_async_remote_copy(
            src_ref=piece_send.at[e, core],
            dst_ref=piece_recv.at[slot],
            send_sem=piece_sems.at[0],
            recv_sem=piece_sems.at[1],
            device_id=(target, me_cls),
            device_id_type=MESH,
        ).start()

    for step in range(tiles):
        pieces(step)
        if step in (2, 4, 6):
            for done in range(step - 2 if step == 2 else step - 1, step + 1):
                sent = lax.rem(my_chip + 1 + done, tiles)
                for part in range(2):
                    for core in range(2):
                        piece_start(part * tiles + sent, core)
    other = lax.rem(my_chip + tiles, 2 * tiles)
    piece_start(other, 0)
    piece_start(other, 1)
    piece_start(my_chip, 1 - my_core)
    gathered = piece_send[my_chip, my_core]
    pltpu.make_async_copy(piece_recv, piece_recv, piece_sems.at[1]).wait()
    for o in range(n_dp - 1):
        gathered = gathered + piece_recv[o]
    data_ref[...] = gathered[:, :64]
    weight_ref[...] = pltpu.roll(gathered, 64, 1)[:, :32]
    pltpu.make_async_copy(piece_recv, piece_recv, piece_sems.at[0]).wait()


def store(data, weight, evidence, data_out, weight_out, evidence_out, sems):
    copies = [
        pltpu.make_async_copy(data, data_out, sems.at[0]),
        pltpu.make_async_copy(weight, weight_out, sems.at[1]),
        pltpu.make_async_copy(evidence, evidence_out, sems.at[2]),
    ]
    for copy in copies:
        copy.start()
    for copy in copies:
        copy.wait()


def body(particles, ctf, references, noise, rotations, counts):
    slots, coefs = ctf.shape
    classes = references.shape[0]
    n_dp = lax.axis_size("dp")
    n_cls = lax.axis_size("cls")
    trig = jnp.asarray(np.stack(phase_tables(coefs), axis=1))
    rows = (SHIFTS + 1) * slots
    pair_count = classes * TURNS
    vmem = pl.BlockSpec(memory_space=pltpu.VMEM)
    data, weight, evidence = pl.pallas_call(
        functools.partial(kernel, (n_dp, n_cls, slots, coefs)),
        out_shape=(
            jax.ShapeDtypeStruct((classes, 2 * coefs // n_dp), jnp.float32),
            jax.ShapeDtypeStruct((classes, coefs // n_dp), jnp.float32),
            jax.ShapeDtypeStruct((1, slots), jnp.float32),
        ),
        in_specs=[pl.BlockSpec(memory_space=pltpu.HBM)] * 7,
        out_specs=(vmem, vmem, vmem),
        scratch_shapes=[
            pltpu.SMEM(counts.shape, jnp.int32),
            pltpu.VMEM(particles.shape, jnp.float32),
            pltpu.VMEM(ctf.shape, jnp.float32),
            pltpu.VMEM(references.shape, references.dtype),
            pltpu.VMEM((1, coefs), jnp.float32),
            pltpu.VMEM(rotations.shape, jnp.int32),
            pltpu.VMEM(trig.shape, jnp.float32),
            pltpu.VMEM((slots, 2 * coefs), jnp.float32),
            pltpu.VMEM((slots, coefs), jnp.bfloat16),
            pltpu.VMEM((rows, 2 * coefs), jnp.bfloat16),
            pltpu.VMEM((pair_count, 2 * coefs), jnp.float32),
            pltpu.VMEM((pair_count, rows), jnp.float32),
            pltpu.VMEM((pair_count, 3 * coefs), jnp.float32),
            pltpu.VMEM((TURNS // 2, 2 * coefs // LANES, 8, LANES), jnp.int32),
            pltpu.VMEM((TURNS, 8, coefs), jnp.int32),
            pltpu.VMEM((8, 2 * coefs), jnp.float32),
            pltpu.VMEM((8, LANES), jnp.float32),
            pltpu.VMEM((n_cls - 1, 8, LANES), jnp.float32),
            pltpu.VMEM((n_dp // 2, 8, LANES), jnp.float32),
            pltpu.VMEM((n_dp // 2, 2, 4, LANES), jnp.float32),
            pltpu.VMEM((n_dp - 1, 4, LANES), jnp.float32),
            pltpu.SemaphoreType.DMA((7,)),
            pltpu.SemaphoreType.DMA((2,)),
            pltpu.SemaphoreType.DMA((2,)),
        ],
        compiler_params=pltpu.CompilerParams(
            collective_id=0, has_side_effects=True, vmem_limit_bytes=40 << 20
        ),
        name="class_average",
    )(
        *[
            pltpu.with_memory_space_constraint(x, pltpu.HBM)
            for x in (counts, particles, ctf, references, noise.reshape(1, coefs), rotations, trig)
        ]
    )
    hbm = pl.BlockSpec(memory_space=pltpu.HBM)
    data, weight, evidence = pl.pallas_call(
        store,
        out_shape=tuple(jax.ShapeDtypeStruct(x.shape, x.dtype) for x in (data, weight, evidence)),
        in_specs=[vmem, vmem, vmem],
        out_specs=(hbm, hbm, hbm),
        scratch_shapes=[pltpu.SemaphoreType.DMA((3,))],
        name="store",
    )(*[pltpu.with_memory_space_constraint(x, pltpu.VMEM) for x in (data, weight, evidence)])
    return data, weight, evidence.reshape(slots)


def solution(mesh):
    placed = (P("dp", None), P("dp", None), P("cls", None), P(), P(), P("dp"))
    return jax.shard_map(
        body,
        mesh=mesh,
        in_specs=placed,
        out_specs=(P("cls", "dp"), P("cls", "dp"), P("dp")),
        check_vma=False,
    )
```
